512 devices in a mesh: ctx: 64 (over z, y_hi, core), head: 8 (over x, y_lo).
Axes of the slice: x: 4, y: 8 (y_hi: 4, y_lo: 2; y = y_hi * 2 + y_lo), z: 8, core: 2. Of those that a mesh axis runs over, the one named last changes fastest.
Arguments:
- prompt_latent: bfloat16 [6144, 576], P('ctx'), may hold values from -8 to 8
- prefill_query: bfloat16 [4096, 64, 192], P('ctx', 'head'), may hold values from -12 to 12
- span_start: int32 [1], replicated, may hold values from 0 to 2048
- w_uk: bfloat16 [64, 128, 512], P('head'), may hold values from -0.5 to 0.5
- w_uv: bfloat16 [64, 512, 128], P('head'), may hold values from -0.25 to 0.25
- decode_latent: bfloat16 [256, 256, 576], P(None, 'ctx'), may hold values from -8 to 8
- owner_slot: int32 [256], replicated, may hold values from 0 to 255, each once
- lengths: int32 [256], P('ctx'), may hold values from 1 to 256
- hidden_new: bfloat16 [4, 256, 7168], P(None, 'ctx', 'head'), may hold values from -6 to 6
- decode_query: bfloat16 [4, 256, 64, 192], P(None, 'ctx', 'head'), may hold values from -12 to 12
- w_down: bfloat16 [7168, 576], P('head'), may hold values from -0.0625 to 0.0625
- kv_gain: float32 [512], replicated, may hold values from 0.5 to 1.5
Outputs:
- prefill_out: bfloat16 [4096, 64, 128], P('ctx', 'head')
- decode_out: bfloat16 [4, 256, 64, 128], P(None, 'ctx', 'head')
The draws below stay inside these ranges and needn't reach their ends.
Inputs may be any that keep to these rules, and one draw needn't show every extreme that they name: span_start + 4096 <= 6144. `owner_slot`: each slot once.
All inputs are finite; a program needn't handle non-finite values.
Results may differ from the reference program's by a relative error of at most 0.014.
Values may be sent and summed in bfloat16 or wider, within the bound.
No kernel may reach another device: no remote copies, remote signals or barrier semaphores. Data moves between devices by JAX's collectives and lax.ppermute only.
A program may use at most 128 MiB of HBM per device.

```python
import jax
import jax.numpy as jnp
from jax import lax

D = 7168
HEADS = 64
KV_RANK = 512
ROPE = 64
NOPE = 128
VDIM = 128
STEPS = 4
LAT = 576
CTX = 6144
QTOK = 4096
CAP = 256
REQS = 256


def base_draw(key, shape):
    values = jax.random.truncated_normal(key, -6.0, 6.0, shape, jnp.float32)
    return values


def draw_prompt_latent(key, part):
    values = base_draw(jax.random.fold_in(key, 11), (CTX, LAT))
    return values.astype(jnp.bfloat16)


def draw_decode_latent(key, part):
    values = base_draw(jax.random.fold_in(key, 13), (REQS, CAP, LAT))
    return values.astype(jnp.bfloat16)


def draw_prefill_query(key, part):
    values = base_draw(jax.random.fold_in(key, 12), (QTOK, HEADS, NOPE + ROPE))
    return values.astype(jnp.bfloat16)


def draw_decode_query(key, part):
    values = base_draw(jax.random.fold_in(key, 14), (STEPS, REQS, HEADS, NOPE + ROPE))
    return values.astype(jnp.bfloat16)


def set_ends(entries, key, low, high):
    longest = entries.shape.index(max(entries.shape))
    spots = []
    for shift in (0, 1):
        where = [jax.random.randint(jax.random.fold_in(key, axis), (), 0, length) for axis, length in enumerate(entries.shape)]
        where[longest] = (where[longest] + shift) % entries.shape[longest]
        spots.append(tuple(where))
    return entries.at[spots[0]].set(low).at[spots[1]].set(high)


def shard_levels(own_key, shape, pieces, least, top_value):
    def one(position, parts):
        steps = jax.random.uniform(jax.random.fold_in(jax.random.fold_in(own_key, 6), position), (parts,), jnp.float32, least / len(pieces), top_value / len(pieces))
        return jnp.repeat(jnp.exp(steps), shape[position] // parts).reshape((-1,) + (1,) * (len(shape) - position - 1))

    gain = one(*pieces[0])
    for cut in pieces[1:]:
        gain = gain * one(*cut)
    return gain


def normal_values(stream_key, extent, deviation, bound, cuts=(), kind=jnp.bfloat16):
    entries = deviation * jax.random.normal(stream_key, extent, jnp.float32)
    if cuts:
        entries = entries * shard_levels(stream_key, extent, cuts, -0.22, 0.18)
    return jnp.clip(entries, -bound, bound).astype(kind)


def setup_inputs(seed: int = 0) -> dict:
    seeds = jax.random.split(jax.random.key(seed), 13)
    return {
        "prompt_latent": draw_prompt_latent(jax.random.fold_in(seeds[12], 71), 0),
        "prefill_query": draw_prefill_query(jax.random.fold_in(seeds[12], 71), 0),
        "span_start": jax.random.randint(seeds[2], (1,), 0, CTX - QTOK + 1).astype(jnp.int32),
        "w_uk": normal_values(seeds[3], (HEADS, NOPE, KV_RANK), NOPE ** -0.5, 0.5, ((0, 8),)),
        "w_uv": normal_values(seeds[4], (HEADS, KV_RANK, VDIM), KV_RANK ** -0.5, 0.25, ((0, 8),)),
        "decode_latent": draw_decode_latent(jax.random.fold_in(seeds[12], 71), 0),
        "owner_slot": jax.random.permutation(seeds[6], REQS).astype(jnp.int32),
        "lengths": set_ends(jax.random.randint(seeds[7], (REQS,), 1, CAP + 1), jax.random.fold_in(seeds[7], 1), 1, CAP).astype(jnp.int32),
        "hidden_new": normal_values(seeds[8], (STEPS, REQS, D), 1.0, 6.0, ((1, 64), (2, 8))),
        "decode_query": draw_decode_query(jax.random.fold_in(seeds[12], 71), 0),
        "w_down": normal_values(seeds[10], (D, LAT), D ** -0.5, 0.0625, ((0, 8),)),
        "kv_gain": jnp.clip(1.0 + 0.1 * jax.random.normal(seeds[11], (KV_RANK,), jnp.float32), 0.5, 1.5),
    }


def absorb(query, w_uk, form):
    nope = query[..., :NOPE].astype(jnp.float32)
    absorbed = jnp.einsum(form, nope, w_uk.astype(jnp.float32)).astype(jnp.bfloat16)
    return jnp.concatenate([absorbed, query[..., NOPE:]], axis=-1)

def reference(prompt_latent, prefill_query, span_start, w_uk, w_uv, decode_latent, owner_slot, lengths, hidden_new, decode_query, w_down, kv_gain):
    scale = (NOPE + ROPE) ** (-0.5)
    full_query = absorb(prefill_query, w_uk, 'qhn,hnc->qhc')
    positions = span_start[0] + jnp.arange(QTOK, dtype=jnp.int32)
    allowed = jnp.arange(CTX, dtype=jnp.int32)[None, :] <= positions[:, None]

    def one_head(items):
        rows, w_head = items
        scores = jnp.dot(rows, prompt_latent.T, preferred_element_type=jnp.float32) * scale
        peak = lax.optimization_barrier(jnp.max(jnp.where(allowed, scores, -1e+30), axis=1))
        probs = jnp.where(allowed, jnp.exp(scores - peak[:, None]), 0.0)
        total = lax.optimization_barrier(jnp.sum(probs, axis=1))
        mixed = jnp.dot(probs.astype(jnp.bfloat16), prompt_latent[:, :KV_RANK], preferred_element_type=jnp.float32)
        mixed = (mixed / total[:, None]).astype(jnp.bfloat16)
        return jnp.dot(mixed, w_head, preferred_element_type=jnp.float32).astype(jnp.bfloat16)
    per_head = lax.map(one_head, (jnp.transpose(full_query, (1, 0, 2)), w_uv))
    prefill_out = jnp.transpose(per_head, (1, 0, 2))
    order = jnp.argsort(owner_slot).astype(jnp.int32)
    cache = decode_latent[order]
    raw = jnp.dot(hidden_new.reshape(-1, D), w_down, preferred_element_type=jnp.float32)
    front = raw[:, :KV_RANK]
    factor = lax.rsqrt(lax.optimization_barrier(jnp.mean(front * front, axis=1)) + 1e-06)
    normed = front * factor[:, None] * kv_gain[None, :]
    new_latent = jnp.concatenate([normed, raw[:, KV_RANK:]], axis=1).astype(jnp.bfloat16).reshape(STEPS, REQS, -1)
    query = absorb(decode_query, w_uk, 'srhn,hnc->srhc').astype(jnp.float32)
    cache_f = cache.astype(jnp.float32)
    new_f = new_latent.astype(jnp.float32)
    cache_scores = jnp.einsum('srhc,rjc->srhj', query, cache_f) * scale
    new_scores = jnp.einsum('srhc,trc->srht', query, new_f) * scale
    cache_ok = (jnp.arange(CAP, dtype=jnp.int32)[None, :] < lengths[:, None])[None, :, None, :]
    steps_idx = jnp.arange(STEPS, dtype=jnp.int32)
    new_ok = (steps_idx[None, :] <= steps_idx[:, None])[:, None, None, :]
    peak = jnp.maximum(lax.optimization_barrier(jnp.max(jnp.where(cache_ok, cache_scores, -1e+30), axis=3)), lax.optimization_barrier(jnp.max(jnp.where(new_ok, new_scores, -1e+30), axis=3)))
    cache_p = jnp.where(cache_ok, jnp.exp(cache_scores - peak[..., None]), 0.0)
    new_p = jnp.where(new_ok, jnp.exp(new_scores - peak[..., None]), 0.0)
    total = lax.optimization_barrier(jnp.sum(cache_p, axis=3)) + lax.optimization_barrier(jnp.sum(new_p, axis=3))
    cache_w = cache_p.astype(jnp.bfloat16).astype(jnp.float32)
    new_w = new_p.astype(jnp.bfloat16).astype(jnp.float32)
    mixed = jnp.einsum('srhj,rjc->srhc', cache_w, cache_f[:, :, :KV_RANK]) + jnp.einsum('srht,trc->srhc', new_w, new_f[:, :, :KV_RANK])
    mixed = (mixed / total[..., None]).astype(jnp.bfloat16).astype(jnp.float32)
    decode_out = jnp.einsum('srhc,hcv->srhv', mixed, w_uv.astype(jnp.float32)).astype(jnp.bfloat16)
    return (prefill_out, decode_out)
```

```python
import jax
import jax.numpy as jnp
import numpy as np
from jax import lax
from jax.experimental import pallas as pl
from jax.experimental.pallas import tpu as pltpu
from jax.sharding import Mesh
from jax.sharding import PartitionSpec as P

KV_RANK = 512
ROPE = 64
NOPE = 128
LOG2E = 1.4426950408889634
SCALE = (NOPE + ROPE) ** (-0.5)
CTX = ("z", "yh", "c")
HEAD = ("x", "yl")


def absorb(query, w_uk, form):
    absorbed = jnp.einsum(form, query[..., :NOPE], w_uk, preferred_element_type=jnp.float32).astype(
        jnp.bfloat16
    )
    return jnp.concatenate([absorbed, query[..., NOPE:]], axis=-1)


def split3(v):
    hi = v.astype(jnp.bfloat16)
    rest = v - hi.astype(jnp.float32)
    mid = rest.astype(jnp.bfloat16)
    low = (rest - mid.astype(jnp.float32)).astype(jnp.bfloat16)
    return hi, mid, low


def flash_kernel(info, q_ref, k1_ref, k2_ref, wuk_ref, wuv_ref, out_ref):
    heads = q_ref.shape[0]
    count = heads * 64
    qbase, own, other = info[0], info[1], info[2]
    rows = []
    for h in range(heads):
        nope = q_ref[h, :64, :]
        pair = q_ref[h, 64:, :]
        rope = jnp.concatenate([pair[:, :64], pair[:, 64:]], axis=0)
        a = jnp.dot(nope, wuk_ref[h], preferred_element_type=jnp.float32).astype(jnp.bfloat16)
        rows.append(jnp.concatenate([a, rope], axis=1))
    full = jnp.concatenate(rows, axis=0)
    qpos = qbase + (lax.broadcasted_iota(jnp.int32, (count, 1), 0) & 63)
    j = lax.broadcasted_iota(jnp.int32, (1, 768), 1)
    blk = (j * 683) >> 16
    kpos = blk * 768 + (j - blk * 96)
    nt = (((1,), (1,)), ((), ()))

    def scores(k_ref, shift):
        s = lax.dot_general(full, k_ref[...], nt, preferred_element_type=jnp.float32)
        return jnp.where(kpos + shift <= qpos, s, -1e30)

    s1 = scores(k1_ref, own)
    s2 = scores(k2_ref, other)
    top = jnp.maximum(jnp.max(s1, axis=1, keepdims=True), jnp.max(s2, axis=1, keepdims=True))
    c = SCALE * LOG2E
    p1 = jnp.exp2((s1 - top) * c)
    p2 = jnp.exp2((s2 - top) * c)
    total = jnp.sum(p1, axis=1, keepdims=True) + jnp.sum(p2, axis=1, keepdims=True)
    acc = jnp.dot(p1.astype(jnp.bfloat16), k1_ref[:, :KV_RANK], preferred_element_type=jnp.float32)
    acc = acc + jnp.dot(
        p2.astype(jnp.bfloat16), k2_ref[:, :KV_RANK], preferred_element_type=jnp.float32
    )
    mixed = (acc / total).astype(jnp.bfloat16)
    for h in range(heads):
        o = jnp.dot(mixed[h * 64 : (h + 1) * 64], wuv_ref[h], preferred_element_type=jnp.float32)
        out_ref[h * 64 : (h + 1) * 64, :] = o.astype(jnp.bfloat16)
    lse = top * c + jnp.log2(total)
    flat = jnp.transpose(jnp.broadcast_to(lse, (count, 128)))[0:1, :]
    lines = jnp.concatenate([flat[:, i * 128 : (i + 1) * 128] for i in range(4)], axis=0)
    hi, mid, low = split3(lines)
    out_ref[count:, :] = jnp.concatenate([hi, mid, low, jnp.zeros_like(hi)], axis=0)


def flash(info, q, k1, k2, w_uk, w_uv):
    vm = pl.BlockSpec(memory_space=pltpu.VMEM)
    return pl.pallas_call(
        flash_kernel,
        out_shape=jax.ShapeDtypeStruct((512 + 16, 128), jnp.bfloat16),
        in_specs=[pl.BlockSpec(memory_space=pltpu.SMEM)] + [vm] * 5,
        out_specs=vm,
        compiler_params=pltpu.CompilerParams(vmem_limit_bytes=48 << 20),
        cost_estimate=pl.CostEstimate(
            flops=2 * 512 * 1536 * 1100, bytes_accessed=6 << 20, transcendentals=512 * 1536
        ),
        name="flash",
    )(info, q, k1, k2, w_uk, w_uv)


def merge_kernel(a_ref, b_ref, c_ref, d_ref, out_ref):
    parts = [a_ref, b_ref, c_ref, d_ref]
    weights = []
    for ref in parts:
        tail = ref[512:, :].astype(jnp.float32)
        lines = tail[0:4] + tail[4:8] + tail[8:12]
        weights.append(lines)
    top = jnp.maximum(jnp.maximum(weights[0], weights[1]), jnp.maximum(weights[2], weights[3]))
    weights = [jnp.exp2(w - top) for w in weights]
    inv = 1.0 / (weights[0] + weights[1] + weights[2] + weights[3])
    weights = [w * inv for w in weights]
    for i in range(4):
        total = jnp.zeros((128, 128), jnp.float32)
        for w, ref in zip(weights, parts):
            col = jnp.transpose(jnp.broadcast_to(w[i : i + 1, :], (128, 128)))
            total = total + col * ref[i * 128 : (i + 1) * 128, :].astype(jnp.float32)
        out_ref[i * 128 : (i + 1) * 128, :] = total.astype(jnp.bfloat16)


def merge(parts):
    vm = pl.BlockSpec(memory_space=pltpu.VMEM)
    return pl.pallas_call(
        merge_kernel,
        out_shape=jax.ShapeDtypeStruct((512, 128), jnp.bfloat16),
        in_specs=[vm] * 4,
        out_specs=vm,
        cost_estimate=pl.CostEstimate(flops=1 << 20, bytes_accessed=1 << 20, transcendentals=4096),
        name="merge",
    )(*parts)


def shift(v, axis, k, n):
    return lax.ppermute(v, axis, [(i, (i + k) % n) for i in range(n)])


def copies(v, n):
    return jnp.broadcast_to(v[None], (n,) + v.shape)


def body(
    prompt_latent,
    prefill_query,
    span_start,
    w_uk,
    w_uv,
    decode_latent,
    owner_slot,
    lengths,
    hidden_new,
    decode_query,
    w_down,
    kv_gain,
):
    heads_here = w_uk.shape[0]
    queries = prefill_query.shape[0]
    width = prompt_latent.shape[1]
    z, yh, c = lax.axis_index("z"), lax.axis_index("yh"), lax.axis_index("c")

    keys = lax.all_to_all(copies(prompt_latent, 8), "z", 0, 0, tiled=True).reshape(768, width)
    other_keys = shift(keys, "c", 1, 2)

    by_head = jnp.transpose(prefill_query, (1, 0, 2))
    rope = by_head[:, :, NOPE:]
    packed = jnp.concatenate(
        [by_head[:, :, :NOPE], jnp.concatenate([rope[:, :32], rope[:, 32:]], axis=2)], axis=1
    )
    parts = [None] * 4
    visiting = [packed] + [shift(packed, "yh", k, 4) for k in (1, 2, 3)]
    for k in (2, 1, 3, 0):
        source = (yh + (4 - k)) & 3
        info = jnp.stack(
            [
                span_start[0] + ((z * 4 + source) * 2 + c) * queries,
                yh * 192 + c * 96,
                yh * 192 + (1 - c) * 96,
            ]
        ).astype(jnp.int32)
        piece = flash(info, visiting[k], keys, other_keys, w_uk, w_uv)
        parts[k] = shift(piece, "yh", 4 - k, 4) if k else piece
    merged = merge(parts)
    prefill_out = jnp.transpose(merged.reshape(heads_here, queries, 128), (1, 0, 2))

    scale = SCALE
    order = jnp.argsort(owner_slot)
    by_slot = decode_latent[order]
    cache = lax.all_to_all(by_slot, CTX, split_axis=0, concat_axis=1, tiled=True)
    steps_here, owned, model_cols = hidden_new.shape
    raw_part = jnp.dot(
        hidden_new.reshape(steps_here * owned, model_cols),
        w_down,
        preferred_element_type=jnp.float32,
    )
    raw = lax.all_to_all(copies(raw_part.astype(jnp.bfloat16), 8), HEAD, 0, 0, tiled=True)
    raw = raw.astype(jnp.float32).sum(0)
    front = raw[:, :KV_RANK]
    factor = lax.rsqrt(jnp.mean(front * front, axis=1) + 1e-06)
    normed = front * factor[:, None] * kv_gain[None, :]
    new_rows = jnp.concatenate([normed, raw[:, KV_RANK:]], axis=1).astype(jnp.bfloat16)
    new_latent = new_rows.reshape(steps_here, owned, width)
    query = absorb(decode_query, w_uk, "srhn,hnc->srhc")
    cache_scores = (
        jnp.einsum("srhc,rjc->srhj", query, cache, preferred_element_type=jnp.float32) * scale
    )
    new_scores = (
        jnp.einsum("srhc,trc->srht", query, new_latent, preferred_element_type=jnp.float32) * scale
    )
    capacity = cache.shape[1]
    cache_ok = (jnp.arange(capacity, dtype=jnp.int32)[None, :] < lengths[:, None])[None, :, None, :]
    steps_idx = jnp.arange(steps_here, dtype=jnp.int32)
    new_ok = (steps_idx[None, :] <= steps_idx[:, None])[:, None, None, :]
    peak = jnp.maximum(
        jnp.max(jnp.where(cache_ok, cache_scores, -1e30), axis=3),
        jnp.max(jnp.where(new_ok, new_scores, -1e30), axis=3),
    )
    cache_p = jnp.where(cache_ok, jnp.exp(cache_scores - peak[..., None]), 0.0)
    new_p = jnp.where(new_ok, jnp.exp(new_scores - peak[..., None]), 0.0)
    total_d = jnp.sum(cache_p, axis=3) + jnp.sum(new_p, axis=3)
    mixed_d = jnp.einsum(
        "srhj,rjc->srhc",
        cache_p.astype(jnp.bfloat16),
        cache[:, :, :KV_RANK],
        preferred_element_type=jnp.float32,
    )
    mixed_d = mixed_d + jnp.einsum(
        "srht,trc->srhc",
        new_p.astype(jnp.bfloat16),
        new_latent[:, :, :KV_RANK],
        preferred_element_type=jnp.float32,
    )
    mixed_d = (mixed_d / total_d[..., None]).astype(jnp.bfloat16)
    decode_out = jnp.einsum(
        "srhc,hcv->srhv", mixed_d, w_uv, preferred_element_type=jnp.float32
    ).astype(jnp.bfloat16)
    return (prefill_out, decode_out)


def solution(mesh):
    fine = Mesh(mesh.devices.reshape(8, 4, 2, 4, 2), ("z", "yh", "c", "x", "yl"))
    in_specs = (
        P(CTX, None),
        P(CTX, HEAD, None),
        P(),
        P(HEAD, None, None),
        P(HEAD, None, None),
        P(None, CTX, None),
        P(),
        P(CTX),
        P(None, CTX, HEAD),
        P(None, CTX, HEAD, None),
        P(HEAD, None),
        P(),
    )
    out_specs = (P(CTX, HEAD, None), P(None, CTX, HEAD, None))
    return jax.shard_map(body, mesh=fine, in_specs=in_specs, out_specs=out_specs, check_vma=False)
```

```python
import jax
import jax.numpy as jnp
import numpy as np
from jax import lax
from jax.experimental import pallas as pl
from jax.experimental.pallas import tpu as pltpu
from jax.sharding import Mesh
from jax.sharding import PartitionSpec as P

KV_RANK = 512
ROPE = 64
NOPE = 128
LOG2E = 1.4426950408889634
SCALE = (NOPE + ROPE) ** (-0.5)
CTX = ("z", "yh", "c")
HEAD = ("x", "yl")


def split3(v):
    hi = v.astype(jnp.bfloat16)
    rest = v - hi.astype(jnp.float32)
    mid = rest.astype(jnp.bfloat16)
    low = (rest - mid.astype(jnp.float32)).astype(jnp.bfloat16)
    return hi, mid, low


def flash_kernel(info, q_ref, k1_ref, k2_ref, wuk_ref, wuv_ref, out_ref):
    heads = q_ref.shape[0]
    count = heads * 64
    qbase, own, other = info[0], info[1], info[2]
    rows = []
    for h in range(heads):
        nope = q_ref[h, :64, :]
        pair = q_ref[h, 64:, :]
        rope = jnp.concatenate([pair[:, :64], pair[:, 64:]], axis=0)
        a = jnp.dot(nope, wuk_ref[h], preferred_element_type=jnp.float32).astype(jnp.bfloat16)
        rows.append(jnp.concatenate([a, rope], axis=1))
    full = jnp.concatenate(rows, axis=0)
    qpos = qbase + (lax.broadcasted_iota(jnp.int32, (count, 1), 0) & 63)
    j = lax.broadcasted_iota(jnp.int32, (1, 768), 1)
    blk = (j * 683) >> 16
    kpos = blk * 768 + (j - blk * 96)
    nt = (((1,), (1,)), ((), ()))

    def scores(k_ref, shift):
        s = lax.dot_general(full, k_ref[...].reshape(768, 576), nt, preferred_element_type=jnp.float32)
        return jnp.where(kpos + shift <= qpos, s, -1e30)

    s1 = scores(k1_ref, own)
    s2 = scores(k2_ref, other)
    top = jnp.maximum(jnp.max(s1, axis=1, keepdims=True), jnp.max(s2, axis=1, keepdims=True))
    c = SCALE * LOG2E
    p1 = jnp.exp2((s1 - top) * c)
    p2 = jnp.exp2((s2 - top) * c)
    total = jnp.sum(p1, axis=1, keepdims=True) + jnp.sum(p2, axis=1, keepdims=True)
    acc = jnp.dot(p1.astype(jnp.bfloat16), k1_ref[...].reshape(768, 576)[:, :KV_RANK], preferred_element_type=jnp.float32)
    acc = acc + jnp.dot(
        p2.astype(jnp.bfloat16), k2_ref[...].reshape(768, 576)[:, :KV_RANK], preferred_element_type=jnp.float32
    )
    mixed = (acc / total).astype(jnp.bfloat16)
    for h in range(heads):
        o = jnp.dot(mixed[h * 64 : (h + 1) * 64], wuv_ref[h], preferred_element_type=jnp.float32)
        out_ref[h * 64 : (h + 1) * 64, :] = o.astype(jnp.bfloat16)
    lse = top * c + jnp.log2(total)
    flat = jnp.transpose(jnp.broadcast_to(lse, (count, 128)))[0:1, :]
    lines = jnp.concatenate([flat[:, i * 128 : (i + 1) * 128] for i in range(4)], axis=0)
    hi, mid, low = split3(lines)
    out_ref[count:, :] = jnp.concatenate([hi, mid, low, jnp.zeros_like(hi)], axis=0)


def flash(info, q, k1, k2, w_uk, w_uv):
    vm = pl.BlockSpec(memory_space=pltpu.VMEM)
    return pl.pallas_call(
        flash_kernel,
        out_shape=jax.ShapeDtypeStruct((512 + 16, 128), jnp.bfloat16),
        in_specs=[pl.BlockSpec(memory_space=pltpu.SMEM)] + [vm] * 5,
        out_specs=vm,
        compiler_params=pltpu.CompilerParams(vmem_limit_bytes=24 << 20),
        cost_estimate=pl.CostEstimate(
            flops=2 * 512 * 1536 * 1100, bytes_accessed=6 << 20, transcendentals=512 * 1536
        ),
        name="flash",
    )(info, q, k1, k2, w_uk, w_uv)


def merge_kernel(a_ref, b_ref, c_ref, d_ref, out_ref):
    parts = [a_ref, b_ref, c_ref, d_ref]
    weights = []
    for ref in parts:
        tail = ref[512:, :].astype(jnp.float32)
        weights.append(tail[0:4] + tail[4:8] + tail[8:12])
    top = jnp.maximum(jnp.maximum(weights[0], weights[1]), jnp.maximum(weights[2], weights[3]))
    weights = [jnp.exp2(w - top) for w in weights]
    inv = 1.0 / (weights[0] + weights[1] + weights[2] + weights[3])
    weights = [w * inv for w in weights]
    merged = []
    for i in range(4):
        total = jnp.zeros((128, 128), jnp.float32)
        for w, ref in zip(weights, parts):
            col = jnp.transpose(jnp.broadcast_to(w[i : i + 1, :], (128, 128)))
            total = total + col * ref[i * 128 : (i + 1) * 128, :].astype(jnp.float32)
        merged.append(total.astype(jnp.bfloat16))
    by_head = jnp.concatenate(merged, axis=0)
    row = lax.broadcasted_iota(jnp.int32, (512, 512), 0)
    col = lax.broadcasted_iota(jnp.int32, (512, 512), 1)
    pick = jnp.where(((row & 7) * 64 + (row >> 3)) == col, 1.0, 0.0).astype(jnp.bfloat16)
    out_ref[...] = jnp.dot(pick, by_head, preferred_element_type=jnp.float32).astype(jnp.bfloat16)


def small(kernel, outs, ins, scalars=0, scratch=(), limit=10, flops=1 << 27, name=None):
    vm = pl.BlockSpec(memory_space=pltpu.VMEM)
    sm = pl.BlockSpec(memory_space=pltpu.SMEM)
    return pl.pallas_call(
        kernel,
        out_shape=outs,
        in_specs=[sm] * scalars + [vm] * (len(ins) - scalars),
        out_specs=jax.tree.map(lambda _: vm, outs),
        scratch_shapes=scratch,
        compiler_params=pltpu.CompilerParams(vmem_limit_bytes=limit << 20),
        cost_estimate=pl.CostEstimate(flops=flops, bytes_accessed=1 << 20, transcendentals=1 << 12),
        name=name,
    )(*ins)


def merge(parts):
    return small(merge_kernel, jax.ShapeDtypeStruct((512, 128), jnp.bfloat16), parts, name="merge")


NT = (((1,), (1,)), ((), ()))


def head_rows(count):
    return lax.broadcasted_iota(jnp.int32, (count, 1), 0) & 7


def prep_kernel(info, q_ref, wuk_ref, hid_ref, wd_ref, *refs):
    outs, rows = refs[:4], refs[4]
    q = q_ref[...].reshape(128, NOPE + ROPE)
    nope = q[:, :NOPE].astype(jnp.float32)
    head = head_rows(128)
    acc = jnp.zeros((128, KV_RANK), jnp.float32)
    for h in range(8):
        mine = jnp.where(head == h, nope, 0.0).astype(jnp.bfloat16)
        acc = acc + jnp.dot(mine, wuk_ref[h], preferred_element_type=jnp.float32)
    rows[:128, :KV_RANK] = acc
    rows[:128, KV_RANK:] = q[:, NOPE:].astype(jnp.float32)
    hidden = jnp.concatenate([hid_ref[t].astype(jnp.float32) for t in range(4)], axis=0)
    raw = lax.dot_general(
        hidden.astype(jnp.bfloat16), wd_ref[...], NT, preferred_element_type=jnp.float32
    ).astype(jnp.bfloat16)
    o = lax.broadcasted_iota(jnp.int32, (32, 16), 0)
    n = lax.broadcasted_iota(jnp.int32, (32, 16), 1)
    pick = jnp.where(((o & 7) * 4 + (o >> 3) == n) & ((o & 7) < 4), 1.0, 0.0)
    rows[128:, :] = jnp.dot(pick.astype(jnp.bfloat16), raw, preferred_element_type=jnp.float32)
    for k in range(4):
        r = (info[0] + k) & 3
        for s in range(4):
            at = pl.multiple_of((s * 4 + r) * 8, 8)
            outs[k][s * 8 : s * 8 + 8, :] = rows[pl.ds(at, 8), :].astype(jnp.bfloat16)
        at = pl.multiple_of(128 + r * 8, 8)
        outs[k][32:40, :] = rows[pl.ds(at, 8), :].astype(jnp.bfloat16)


def pack_kernel(info, owner_ref, x_ref, out_ref):
    row = lax.broadcasted_iota(jnp.int32, (256, 256), 0)
    hit = owner_ref[...] == ((row >> 2) * 4 + info[0])
    acc = jnp.zeros((256, KV_RANK + ROPE), jnp.float32)
    for j in range(4):
        pick = jnp.where(hit & ((row & 3) == j), 1.0, 0.0).astype(jnp.bfloat16)
        acc = acc + lax.dot_general(pick, x_ref[j], NT, preferred_element_type=jnp.float32)
    out_ref[...] = acc.astype(jnp.bfloat16)


def attend_kernel(info, p0, p1, p2, p3, raw_a, raw_b, cache_ref, gain_ref, out_ref):
    raw = raw_a[...] + raw_b[...]
    front = raw[:, :KV_RANK]
    factor = lax.rsqrt(jnp.mean(front * front, axis=1, keepdims=True) + 1e-06)
    fresh = jnp.concatenate([front * factor * gain_ref[...], raw[:, KV_RANK:]], axis=1)
    fresh = fresh.astype(jnp.bfloat16)
    q = jnp.concatenate([p[:32, :] for p in (p0, p1, p2, p3)], axis=0)
    cache = cache_ref[...]
    s1 = lax.dot_general(q, cache, NT, preferred_element_type=jnp.float32)
    s2 = lax.dot_general(q, fresh, NT, preferred_element_type=jnp.float32)
    j = lax.broadcasted_iota(jnp.int32, (128, 256), 1)
    s1 = jnp.where(j < info[1], s1, -1e30)
    step = (lax.broadcasted_iota(jnp.int32, (128, 8), 0) >> 3) & 3
    s2 = jnp.where(lax.broadcasted_iota(jnp.int32, (128, 8), 1) <= step, s2, -1e30)
    top = jnp.maximum(jnp.max(s1, axis=1, keepdims=True), jnp.max(s2, axis=1, keepdims=True))
    c = SCALE * LOG2E
    p_c = jnp.exp2((s1 - top) * c)
    p_n = jnp.exp2((s2 - top) * c)
    total = jnp.sum(p_c, axis=1, keepdims=True) + jnp.sum(p_n, axis=1, keepdims=True)
    acc = jnp.dot(p_c.astype(jnp.bfloat16), cache[:, :KV_RANK], preferred_element_type=jnp.float32)
    acc = acc + jnp.dot(
        p_n.astype(jnp.bfloat16), fresh[:, :KV_RANK], preferred_element_type=jnp.float32
    )
    mixed = (acc / total).astype(jnp.bfloat16)
    for k in range(4):
        out_ref[(info[0] - k) & 3] = mixed[k * 32 : (k + 1) * 32]


def finish_kernel(m_ref, wuv_ref, out_ref):
    m = m_ref[...].reshape(128, KV_RANK).astype(jnp.float32)
    head = head_rows(128)
    acc = jnp.zeros((128, 128), jnp.float32)
    for h in range(8):
        mine = jnp.where(head == h, m, 0.0).astype(jnp.bfloat16)
        acc = acc + jnp.dot(mine, wuv_ref[h], preferred_element_type=jnp.float32)
    for r in range(4):
        for s in range(4):
            at = (r * 4 + s) * 8
            out_ref[s, r] = acc[at : at + 8].astype(jnp.bfloat16)


def shift(v, axis, k, n):
    return lax.ppermute(v, axis, [(i, (i + k) % n) for i in range(n)])


def copies(v, n):
    return jnp.broadcast_to(v[None], (n,) + v.shape)


def body(
    prompt_latent,
    prefill_query,
    span_start,
    w_uk,
    w_uv,
    decode_latent,
    owner_slot,
    lengths,
    hidden_new,
    decode_query,
    w_down,
    kv_gain,
):
    heads_here = w_uk.shape[0]
    queries = prefill_query.shape[0]
    width = prompt_latent.shape[1]
    z, yh, c = lax.axis_index("z"), lax.axis_index("yh"), lax.axis_index("c")

    keys = lax.all_to_all(copies(prompt_latent, 8), "z", 0, 0, tiled=True)
    other_keys = shift(keys, "c", 1, 2)

    by_head = jnp.transpose(prefill_query, (1, 0, 2))
    rope = by_head[:, :, NOPE:]
    packed = jnp.concatenate(
        [by_head[:, :, :NOPE], jnp.concatenate([rope[:, :32], rope[:, 32:]], axis=2)], axis=1
    )
    parts = [None] * 4
    visiting = [packed] + [shift(packed, "yh", k, 4) for k in (1, 2, 3)]
    for k in (2, 1, 3, 0):
        source = (yh + (4 - k)) & 3
        info = jnp.stack(
            [
                span_start[0] + ((z * 4 + source) * 2 + c) * queries,
                yh * 192 + c * 96,
                yh * 192 + (1 - c) * 96,
            ]
        ).astype(jnp.int32)
        piece = flash(info, visiting[k], keys, other_keys, w_uk, w_uv)
        parts[k] = shift(piece, "yh", 4 - k, 4) if k else piece
    merged = merge(parts)
    prefill_out = merged.reshape(queries, heads_here, 128)

    x = lax.axis_index("x").astype(jnp.int32)
    bf = jnp.bfloat16
    tile = jax.ShapeDtypeStruct((40, width), bf)
    sent = small(
        prep_kernel,
        [tile] * 4,
        [x.reshape(1), decode_query, w_uk, hidden_new, w_down.T],
        1,
        [pltpu.VMEM((160, width), jnp.float32)],
        name="prep",
    )
    got = [sent[0]] + [shift(sent[k], "x", k, 4) for k in (1, 2, 3)]
    raw_here = got[0][32:].astype(jnp.float32)
    for k in (1, 2, 3):
        raw_here = raw_here + got[k][32:].astype(jnp.float32)
    raw_there = shift(raw_here, "yl", 1, 2)
    rows = small(
        pack_kernel,
        jax.ShapeDtypeStruct((256, width), bf),
        [x.reshape(1), owner_slot.reshape(1, 256), jnp.transpose(decode_latent, (1, 2, 0))],
        1,
        name="pack",
    )
    cache = lax.all_to_all(rows.reshape(64, 4, width), CTX, 0, 0, tiled=True).reshape(256, width)
    own_length = lax.dynamic_slice(lengths, (x,), (1,))
    mixed = small(
        attend_kernel,
        jax.ShapeDtypeStruct((4, 32, KV_RANK), bf),
        [
            jnp.concatenate([x.reshape(1), own_length]),
            *got,
            raw_here,
            raw_there,
            cache,
            kv_gain.reshape(1, KV_RANK),
        ],
        1,
        name="attend",
    )
    mixed = lax.all_to_all(mixed, "x", 0, 0, tiled=True)
    decode_out = small(
        finish_kernel,
        jax.ShapeDtypeStruct((4, 4, 8, 128), bf),
        [mixed, w_uv],
        name="finish",
    )
    return (prefill_out, decode_out)


def solution(mesh):
    fine = Mesh(mesh.devices.reshape(8, 4, 2, 4, 2), ("z", "yh", "c", "x", "yl"))
    in_specs = (
        P(CTX, None),
        P(CTX, HEAD, None),
        P(),
        P(HEAD, None, None),
        P(HEAD, None, None),
        P(None, CTX, None),
        P(),
        P(CTX),
        P(None, CTX, HEAD),
        P(None, CTX, HEAD, None),
        P(HEAD, None),
        P(),
    )
    out_specs = (P(CTX, HEAD, None), P(None, CTX, HEAD, None))
    return jax.shard_map(body, mesh=fine, in_specs=in_specs, out_specs=out_specs, check_vma=False)
```

```python
import jax
import jax.numpy as jnp
import numpy as np
from jax import lax
from jax.experimental import pallas as pl
from jax.experimental.pallas import tpu as pltpu
from jax.sharding import Mesh
from jax.sharding import PartitionSpec as P

KV_RANK = 512
ROPE = 64
NOPE = 128
LOG2E = 1.4426950408889634
SCALE = (NOPE + ROPE) ** (-0.5)
CTX = ("z", "yh", "c")
HEAD = ("x", "yl")


def split3(v):
    hi = v.astype(jnp.bfloat16)
    rest = v - hi.astype(jnp.float32)
    mid = rest.astype(jnp.bfloat16)
    low = (rest - mid.astype(jnp.float32)).astype(jnp.bfloat16)
    return hi, mid, low


def flash_kernel(info, q_ref, k1_ref, k2_ref, wuk_ref, wuv_ref, out_ref):
    heads = q_ref.shape[0]
    count = heads * 64
    qbase, own, other = info[0], info[1], info[2]
    rows = []
    for h in range(heads):
        nope = q_ref[h, :64, :]
        pair = q_ref[h, 64:, :]
        rope = jnp.concatenate([pair[:, :64], pair[:, 64:]], axis=0)
        a = jnp.dot(nope, wuk_ref[h], preferred_element_type=jnp.float32).astype(jnp.bfloat16)
        rows.append(jnp.concatenate([a, rope], axis=1))
    full = jnp.concatenate(rows, axis=0)
    qpos = qbase + (lax.broadcasted_iota(jnp.int32, (count, 1), 0) & 63)
    j = lax.broadcasted_iota(jnp.int32, (1, 768), 1)
    blk = (j * 683) >> 16
    kpos = blk * 768 + (j - blk * 96)
    nt = (((1,), (1,)), ((), ()))

    def scores(k_ref, shift):
        s = lax.dot_general(full, k_ref[...].reshape(768, 576), nt, preferred_element_type=jnp.float32)
        return jnp.where(kpos + shift <= qpos, s, -1e30)

    s1 = scores(k1_ref, own)
    s2 = scores(k2_ref, other)
    top = jnp.maximum(jnp.max(s1, axis=1, keepdims=True), jnp.max(s2, axis=1, keepdims=True))
    c = SCALE * LOG2E
    p1 = jnp.exp2((s1 - top) * c)
    p2 = jnp.exp2((s2 - top) * c)
    total = jnp.sum(p1, axis=1, keepdims=True) + jnp.sum(p2, axis=1, keepdims=True)
    acc = jnp.dot(p1.astype(jnp.bfloat16), k1_ref[...].reshape(768, 576)[:, :KV_RANK], preferred_element_type=jnp.float32)
    acc = acc + jnp.dot(
        p2.astype(jnp.bfloat16), k2_ref[...].reshape(768, 576)[:, :KV_RANK], preferred_element_type=jnp.float32
    )
    mixed = (acc / total).astype(jnp.bfloat16)
    for h in range(heads):
        o = jnp.dot(mixed[h * 64 : (h + 1) * 64], wuv_ref[h], preferred_element_type=jnp.float32)
        out_ref[h * 64 : (h + 1) * 64, :] = o.astype(jnp.bfloat16)
    lse = top * c + jnp.log2(total)
    flat = jnp.transpose(jnp.broadcast_to(lse, (count, 128)))[0:1, :]
    lines = jnp.concatenate([flat[:, i * 128 : (i + 1) * 128] for i in range(4)], axis=0)
    hi, mid, low = split3(lines)
    out_ref[count:, :] = jnp.concatenate([hi, mid, low, jnp.zeros_like(hi)], axis=0)


def flash(info, q, k1, k2, w_uk, w_uv):
    vm = pl.BlockSpec(memory_space=pltpu.VMEM)
    return pl.pallas_call(
        flash_kernel,
        out_shape=jax.ShapeDtypeStruct((512 + 16, 128), jnp.bfloat16),
        in_specs=[pl.BlockSpec(memory_space=pltpu.SMEM)] + [vm] * 5,
        out_specs=vm,
        compiler_params=pltpu.CompilerParams(vmem_limit_bytes=24 << 20),
        cost_estimate=pl.CostEstimate(
            flops=2 * 512 * 1536 * 1100, bytes_accessed=6 << 20, transcendentals=512 * 1536
        ),
        name="flash",
    )(info, q, k1, k2, w_uk, w_uv)


def merge_kernel(a_ref, b_ref, c_ref, d_ref, out_ref):
    parts = [a_ref, b_ref, c_ref, d_ref]
    weights = []
    for ref in parts:
        tail = ref[512:, :].astype(jnp.float32)
        weights.append(tail[0:4] + tail[4:8] + tail[8:12])
    top = jnp.maximum(jnp.maximum(weights[0], weights[1]), jnp.maximum(weights[2], weights[3]))
    weights = [jnp.exp2(w - top) for w in weights]
    inv = 1.0 / (weights[0] + weights[1] + weights[2] + weights[3])
    weights = [w * inv for w in weights]
    merged = []
    for i in range(4):
        total = jnp.zeros((128, 128), jnp.float32)
        for w, ref in zip(weights, parts):
            col = jnp.transpose(jnp.broadcast_to(w[i : i + 1, :], (128, 128)))
            total = total + col * ref[i * 128 : (i + 1) * 128, :].astype(jnp.float32)
        merged.append(total.astype(jnp.bfloat16))
    by_head = jnp.concatenate(merged, axis=0)
    row = lax.broadcasted_iota(jnp.int32, (512, 512), 0)
    col = lax.broadcasted_iota(jnp.int32, (512, 512), 1)
    pick = jnp.where(((row & 7) * 64 + (row >> 3)) == col, 1.0, 0.0).astype(jnp.bfloat16)
    out_ref[...] = jnp.dot(pick, by_head, preferred_element_type=jnp.float32).astype(jnp.bfloat16)


def small(kernel, outs, ins, scalars=0, scratch=(), limit=10, flops=1 << 27, name=None):
    vm = pl.BlockSpec(memory_space=pltpu.VMEM)
    sm = pl.BlockSpec(memory_space=pltpu.SMEM)
    return pl.pallas_call(
        kernel,
        out_shape=outs,
        in_specs=[sm] * scalars + [vm] * (len(ins) - scalars),
        out_specs=jax.tree.map(lambda _: vm, outs),
        scratch_shapes=scratch,
        compiler_params=pltpu.CompilerParams(vmem_limit_bytes=limit << 20),
        cost_estimate=pl.CostEstimate(flops=flops, bytes_accessed=1 << 20, transcendentals=1 << 12),
        name=name,
    )(*ins)


def merge(parts):
    return small(merge_kernel, jax.ShapeDtypeStruct((512, 128), jnp.bfloat16), parts, name="merge")


NT = (((1,), (1,)), ((), ()))


def head_rows(count):
    return lax.broadcasted_iota(jnp.int32, (count, 1), 0) & 7


def prep_kernel(info, q_ref, wuk_ref, hid_ref, wd_ref, *refs):
    outs, rows = refs[:4], refs[4]
    q = q_ref[...].reshape(128, NOPE + ROPE)
    nope = q[:, :NOPE].astype(jnp.float32)
    head = head_rows(128)
    acc = jnp.zeros((128, KV_RANK), jnp.float32)
    for h in range(8):
        mine = jnp.where(head == h, nope, 0.0).astype(jnp.bfloat16)
        acc = acc + jnp.dot(mine, wuk_ref[h], preferred_element_type=jnp.float32)
    rows[:128, :KV_RANK] = acc
    rows[:128, KV_RANK:] = q[:, NOPE:].astype(jnp.float32)
    hidden = jnp.concatenate([hid_ref[t].astype(jnp.float32) for t in range(4)], axis=0)
    raw = lax.dot_general(
        hidden.astype(jnp.bfloat16), wd_ref[...], NT, preferred_element_type=jnp.float32
    ).astype(jnp.bfloat16)
    o = lax.broadcasted_iota(jnp.int32, (32, 16), 0)
    n = lax.broadcasted_iota(jnp.int32, (32, 16), 1)
    pick = jnp.where(((o & 7) * 4 + (o >> 3) == n) & ((o & 7) < 4), 1.0, 0.0)
    rows[128:, :] = jnp.dot(pick.astype(jnp.bfloat16), raw, preferred_element_type=jnp.float32)
    for k in range(4):
        r = (info[0] + k) & 3
        for s in range(4):
            at = pl.multiple_of((s * 4 + r) * 8, 8)
            outs[k][s * 8 : s * 8 + 8, :] = rows[pl.ds(at, 8), :].astype(jnp.bfloat16)
        at = pl.multiple_of(128 + r * 8, 8)
        outs[k][32:40, :] = rows[pl.ds(at, 8), :].astype(jnp.bfloat16)


def pack_kernel(info, owner_ref, x_ref, out_ref):
    row = lax.broadcasted_iota(jnp.int32, (256, 256), 0)
    hit = owner_ref[...] == ((row >> 2) * 4 + info[0])
    acc = jnp.zeros((256, KV_RANK + ROPE), jnp.float32)
    for j in range(4):
        pick = jnp.where(hit & ((row & 3) == j), 1.0, 0.0).astype(jnp.bfloat16)
        acc = acc + lax.dot_general(pick, x_ref[j], NT, preferred_element_type=jnp.float32)
    out_ref[...] = acc.astype(jnp.bfloat16)


def attend_kernel(info, p0, p1, p2, p3, raw_a, raw_b, cache_ref, gain_ref, out_ref):
    raw = raw_a[...] + raw_b[...]
    front = raw[:, :KV_RANK]
    factor = lax.rsqrt(jnp.mean(front * front, axis=1, keepdims=True) + 1e-06)
    fresh = jnp.concatenate([front * factor * gain_ref[...], raw[:, KV_RANK:]], axis=1)
    fresh = fresh.astype(jnp.bfloat16)
    q = jnp.concatenate([p[:32, :] for p in (p0, p1, p2, p3)], axis=0)
    cache = cache_ref[...]
    s1 = lax.dot_general(q, cache, NT, preferred_element_type=jnp.float32)
    s2 = lax.dot_general(q, fresh, NT, preferred_element_type=jnp.float32)
    j = lax.broadcasted_iota(jnp.int32, (128, 256), 1)
    s1 = jnp.where(j < info[1], s1, -1e30)
    step = (lax.broadcasted_iota(jnp.int32, (128, 8), 0) >> 3) & 3
    s2 = jnp.where(lax.broadcasted_iota(jnp.int32, (128, 8), 1) <= step, s2, -1e30)
    top = jnp.maximum(jnp.max(s1, axis=1, keepdims=True), jnp.max(s2, axis=1, keepdims=True))
    c = SCALE * LOG2E
    p_c = jnp.exp2((s1 - top) * c)
    p_n = jnp.exp2((s2 - top) * c)
    total = jnp.sum(p_c, axis=1, keepdims=True) + jnp.sum(p_n, axis=1, keepdims=True)
    acc = jnp.dot(p_c.astype(jnp.bfloat16), cache[:, :KV_RANK], preferred_element_type=jnp.float32)
    acc = acc + jnp.dot(
        p_n.astype(jnp.bfloat16), fresh[:, :KV_RANK], preferred_element_type=jnp.float32
    )
    mixed = (acc / total).astype(jnp.bfloat16)
    for k in range(4):
        out_ref[(info[0] - k) & 3] = mixed[k * 32 : (k + 1) * 32]


def finish_kernel(m_ref, wuv_ref, out_ref):
    m = m_ref[...].reshape(128, KV_RANK).astype(jnp.float32)
    head = head_rows(128)
    acc = jnp.zeros((128, 128), jnp.float32)
    for h in range(8):
        mine = jnp.where(head == h, m, 0.0).astype(jnp.bfloat16)
        acc = acc + jnp.dot(mine, wuv_ref[h], preferred_element_type=jnp.float32)
    for r in range(4):
        for s in range(4):
            at = (r * 4 + s) * 8
            out_ref[s, r] = acc[at : at + 8].astype(jnp.bfloat16)


def shift(v, axis, k, n):
    return lax.ppermute(v, axis, [(i, (i + k) % n) for i in range(n)])


def copies(v, n):
    return jnp.broadcast_to(v[None], (n,) + v.shape)


def body(
    prompt_latent,
    prefill_query,
    span_start,
    w_uk,
    w_uv,
    decode_latent,
    owner_slot,
    lengths,
    hidden_new,
    decode_query,
    w_down,
    kv_gain,
):
    heads_here = w_uk.shape[0]
    queries = prefill_query.shape[0]
    width = prompt_latent.shape[1]
    z, yh, c = lax.axis_index("z"), lax.axis_index("yh"), lax.axis_index("c")

    bf = jnp.bfloat16
    x = lax.axis_index("x").astype(jnp.int32)
    fence = lax.optimization_barrier
    keys = lax.all_to_all(copies(prompt_latent, 8), "z", 0, 0, tiled=True)

    by_head = jnp.transpose(prefill_query, (1, 0, 2))
    rope = by_head[:, :, NOPE:]
    packed = jnp.concatenate(
        [by_head[:, :, :NOPE], jnp.concatenate([rope[:, :32], rope[:, 32:]], axis=2)], axis=1
    )
    visiting = [packed] + [shift(packed, "yh", k, 4) for k in (1, 2, 3)]
    tile = jax.ShapeDtypeStruct((40, width), bf)
    sent = small(
        prep_kernel,
        [tile] * 4,
        [x.reshape(1), decode_query, w_uk, hidden_new, w_down.T],
        1,
        [pltpu.VMEM((160, width), jnp.float32)],
        name="prep",
    )
    got = [sent[0]] + [shift(sent[k], "x", k, 4) for k in (1, 2, 3)]
    raw_here = got[0][32:].astype(jnp.float32)
    for k in (1, 2, 3):
        raw_here = raw_here + got[k][32:].astype(jnp.float32)
    raw_there = shift(raw_here, "yl", 1, 2)
    rows = small(
        pack_kernel,
        jax.ShapeDtypeStruct((256, width), bf),
        [x.reshape(1), owner_slot.reshape(1, 256), jnp.transpose(decode_latent, (1, 2, 0))],
        1,
        name="pack",
    ).reshape(64, 4, width)

    keys, raw_there, rows, *rest = fence((keys, raw_there, rows, *visiting[1:]))
    visiting = [packed] + rest
    other_keys = shift(keys, "c", 1, 2)
    cache = lax.all_to_all(rows, CTX, 0, 0, tiled=True)

    def attention(k, q):
        source = (yh + (4 - k)) & 3
        info = jnp.stack(
            [
                span_start[0] + ((z * 4 + source) * 2 + c) * queries,
                yh * 192 + c * 96,
                yh * 192 + (1 - c) * 96,
            ]
        ).astype(jnp.int32)
        return flash(info, q, keys, other_keys, w_uk, w_uv)

    parts = [None] * 4
    previous = None
    for k in (2, 1, 3):
        q = visiting[k]
        if previous is not None:
            q, previous = fence((q, previous))
        previous = attention(k, q)
        parts[k] = shift(previous, "yh", 4 - k, 4)

    cache, previous = fence((cache, previous))
    own_length = lax.dynamic_slice(lengths, (x,), (1,))
    mixed = small(
        attend_kernel,
        jax.ShapeDtypeStruct((4, 32, KV_RANK), bf),
        [
            jnp.concatenate([x.reshape(1), own_length]),
            *got,
            raw_here,
            raw_there,
            cache.reshape(256, width),
            kv_gain.reshape(1, KV_RANK),
        ],
        1,
        name="attend",
    )
    q, mixed = fence((packed, mixed))
    mixed = lax.all_to_all(mixed, "x", 0, 0, tiled=True)
    parts[0] = attention(0, q)
    mixed, parts[0] = fence((mixed, parts[0]))
    decode_out = small(
        finish_kernel,
        jax.ShapeDtypeStruct((4, 4, 8, 128), bf),
        [mixed, w_uv],
        name="finish",
    )
    prefill_out = merge(parts).reshape(queries, heads_here, 128)
    return (prefill_out, decode_out)


def solution(mesh):
    fine = Mesh(mesh.devices.reshape(8, 4, 2, 4, 2), ("z", "yh", "c", "x", "yl"))
    in_specs = (
        P(CTX, None),
        P(CTX, HEAD, None),
        P(),
        P(HEAD, None, None),
        P(HEAD, None, None),
        P(None, CTX, None),
        P(),
        P(CTX),
        P(None, CTX, HEAD),
        P(None, CTX, HEAD, None),
        P(HEAD, None),
        P(),
    )
    out_specs = (P(CTX, HEAD, None), P(None, CTX, HEAD, None))
    return jax.shard_map(body, mesh=fine, in_specs=in_specs, out_specs=out_specs, check_vma=False)
```

```python
import jax
import jax.numpy as jnp
import numpy as np
from jax import lax
from jax.experimental import pallas as pl
from jax.experimental.pallas import tpu as pltpu
from jax.sharding import Mesh
from jax.sharding import PartitionSpec as P

KV_RANK = 512
ROPE = 64
NOPE = 128
LOG2E = 1.4426950408889634
SCALE = (NOPE + ROPE) ** (-0.5)
CTX = ("z", "yh", "c")
HEAD = ("x", "yl")


def split3(v):
    hi = v.astype(jnp.bfloat16)
    rest = v - hi.astype(jnp.float32)
    mid = rest.astype(jnp.bfloat16)
    low = (rest - mid.astype(jnp.float32)).astype(jnp.bfloat16)
    return hi, mid, low


def flash_kernel(start, q0, q1, q2, q3, k1_ref, k2_ref, wuk_ref, wuv_ref, o0, o1, o2, o3):
    z, yh, c = lax.axis_index("z"), lax.axis_index("yh"), lax.axis_index("c")
    k1 = k1_ref[...].reshape(768, 576)
    k2 = k2_ref[...].reshape(768, 576)
    j = lax.broadcasted_iota(jnp.int32, (1, 768), 1)
    blk = (j * 683) >> 16
    kpos = blk * 768 + (j - blk * 96) + yh * 192
    where1, where2 = kpos + c * 96, kpos + (1 - c) * 96
    scale = SCALE * LOG2E
    queries, outs = (q0, q1, q2, q3), (o0, o1, o2, o3)

    def score(k):
        rows = []
        for h in range(8):
            pair = queries[k][h, 64:, :]
            rope = jnp.concatenate([pair[:, :64], pair[:, 64:]], axis=0)
            a = jnp.dot(queries[k][h, :64, :], wuk_ref[h], preferred_element_type=jnp.float32)
            rows.append(jnp.concatenate([a.astype(jnp.bfloat16), rope], axis=1))
        full = jnp.concatenate(rows, axis=0)
        s1 = lax.dot_general(full, k1, NT, preferred_element_type=jnp.float32)
        s2 = lax.dot_general(full, k2, NT, preferred_element_type=jnp.float32)
        return s1, s2

    def weigh(k, s):
        source = (yh + (4 - k)) & 3
        first = start[0] + ((z * 4 + source) * 2 + c) * 64
        qpos = first + (lax.broadcasted_iota(jnp.int32, (512, 1), 0) & 63)
        s1 = jnp.where(where1 <= qpos, s[0], -1e30)
        s2 = jnp.where(where2 <= qpos, s[1], -1e30)
        top = jnp.maximum(jnp.max(s1, axis=1, keepdims=True), jnp.max(s2, axis=1, keepdims=True))
        p1 = jnp.exp2((s1 - top) * scale)
        p2 = jnp.exp2((s2 - top) * scale)
        total = jnp.sum(p1, axis=1, keepdims=True) + jnp.sum(p2, axis=1, keepdims=True)
        lse = top * scale + jnp.log2(total)
        return p1.astype(jnp.bfloat16), p2.astype(jnp.bfloat16), total, lse

    def mix(k, p1, p2, total, lse):
        acc = jnp.dot(p1, k1[:, :KV_RANK], preferred_element_type=jnp.float32)
        acc = acc + jnp.dot(p2, k2[:, :KV_RANK], preferred_element_type=jnp.float32)
        mixed = (acc / total).astype(jnp.bfloat16)
        for h in range(8):
            at = h * 64
            o = jnp.dot(mixed[at : at + 64], wuv_ref[h], preferred_element_type=jnp.float32)
            outs[k][at : at + 64, :] = o.astype(jnp.bfloat16)
        flat = jnp.transpose(jnp.broadcast_to(lse, (512, 128)))[0:1, :]
        lines = jnp.concatenate([flat[:, i * 128 : (i + 1) * 128] for i in range(4)], axis=0)
        hi, mid, low = split3(lines)
        outs[k][512:, :] = jnp.concatenate([hi, mid, low, jnp.zeros_like(hi)], axis=0)

    s = score(0)
    for k in range(4):
        following = score(k + 1) if k < 3 else None
        mix(k, *weigh(k, s))
        s = following


def merge_kernel(a_ref, b_ref, c_ref, d_ref, out_ref):
    parts = [a_ref, b_ref, c_ref, d_ref]
    weights = []
    for ref in parts:
        tail = ref[512:, :].astype(jnp.float32)
        weights.append(tail[0:4] + tail[4:8] + tail[8:12])
    top = jnp.maximum(jnp.maximum(weights[0], weights[1]), jnp.maximum(weights[2], weights[3]))
    weights = [jnp.exp2(w - top) for w in weights]
    inv = 1.0 / (weights[0] + weights[1] + weights[2] + weights[3])
    weights = [w * inv for w in weights]
    merged = []
    for i in range(4):
        total = jnp.zeros((128, 128), jnp.float32)
        for w, ref in zip(weights, parts):
            col = jnp.transpose(jnp.broadcast_to(w[i : i + 1, :], (128, 128)))
            total = total + col * ref[i * 128 : (i + 1) * 128, :].astype(jnp.float32)
        merged.append(total.astype(jnp.bfloat16))
    by_head = jnp.concatenate(merged, axis=0)
    row = lax.broadcasted_iota(jnp.int32, (512, 512), 0)
    col = lax.broadcasted_iota(jnp.int32, (512, 512), 1)
    pick = jnp.where(((row & 7) * 64 + (row >> 3)) == col, 1.0, 0.0).astype(jnp.bfloat16)
    out_ref[...] = jnp.dot(pick, by_head, preferred_element_type=jnp.float32).astype(jnp.bfloat16)


def small(kernel, outs, ins, scalars=0, scratch=(), limit=10, flops=1 << 27, name=None):
    vm = pl.BlockSpec(memory_space=pltpu.VMEM)
    sm = pl.BlockSpec(memory_space=pltpu.SMEM)
    return pl.pallas_call(
        kernel,
        out_shape=outs,
        in_specs=[sm] * scalars + [vm] * (len(ins) - scalars),
        out_specs=jax.tree.map(lambda _: vm, outs),
        scratch_shapes=scratch,
        compiler_params=pltpu.CompilerParams(vmem_limit_bytes=limit << 20),
        cost_estimate=pl.CostEstimate(flops=flops, bytes_accessed=1 << 20, transcendentals=1 << 12),
        name=name,
    )(*ins)


def merge(parts):
    return small(merge_kernel, jax.ShapeDtypeStruct((512, 128), jnp.bfloat16), parts, name="merge")


NT = (((1,), (1,)), ((), ()))


def head_rows(count):
    return lax.broadcasted_iota(jnp.int32, (count, 1), 0) & 7


def prep_kernel(q_ref, wuk_ref, hid_ref, wd_ref, *refs):
    outs, rows = refs[:4], refs[4]
    q = q_ref[...].reshape(128, NOPE + ROPE)
    nope = q[:, :NOPE].astype(jnp.float32)
    head = head_rows(128)
    acc = jnp.zeros((128, KV_RANK), jnp.float32)
    for h in range(8):
        mine = jnp.where(head == h, nope, 0.0).astype(jnp.bfloat16)
        acc = acc + jnp.dot(mine, wuk_ref[h], preferred_element_type=jnp.float32)
    rows[:128, :KV_RANK] = acc
    rows[:128, KV_RANK:] = q[:, NOPE:].astype(jnp.float32)
    hidden = jnp.concatenate([hid_ref[t].astype(jnp.float32) for t in range(4)], axis=0)
    raw = lax.dot_general(
        hidden.astype(jnp.bfloat16), wd_ref[...], NT, preferred_element_type=jnp.float32
    ).astype(jnp.bfloat16)
    o = lax.broadcasted_iota(jnp.int32, (32, 16), 0)
    n = lax.broadcasted_iota(jnp.int32, (32, 16), 1)
    pick = jnp.where(((o & 7) * 4 + (o >> 3) == n) & ((o & 7) < 4), 1.0, 0.0)
    rows[128:, :] = jnp.dot(pick.astype(jnp.bfloat16), raw, preferred_element_type=jnp.float32)
    for k in range(4):
        r = (lax.axis_index("x") + k) & 3
        for s in range(4):
            at = pl.multiple_of((s * 4 + r) * 8, 8)
            outs[k][s * 8 : s * 8 + 8, :] = rows[pl.ds(at, 8), :].astype(jnp.bfloat16)
        at = pl.multiple_of(128 + r * 8, 8)
        outs[k][32:40, :] = rows[pl.ds(at, 8), :].astype(jnp.bfloat16)


def pack_kernel(owner_ref, x_ref, out_ref):
    row = lax.broadcasted_iota(jnp.int32, (256, 256), 0)
    hit = owner_ref[...] == ((row >> 2) * 4 + lax.axis_index("x"))
    acc = jnp.zeros((256, KV_RANK + ROPE), jnp.float32)
    for j in range(4):
        pick = jnp.where(hit & ((row & 3) == j), 1.0, 0.0).astype(jnp.bfloat16)
        acc = acc + lax.dot_general(pick, x_ref[j], NT, preferred_element_type=jnp.float32)
    out_ref[...] = acc.astype(jnp.bfloat16)


def attend_kernel(lengths, p0, p1, p2, p3, raw_a, raw_b, cache_ref, gain_ref, out_ref):
    raw = raw_a[...] + raw_b[...]
    front = raw[:, :KV_RANK]
    factor = lax.rsqrt(jnp.mean(front * front, axis=1, keepdims=True) + 1e-06)
    fresh = jnp.concatenate([front * factor * gain_ref[...], raw[:, KV_RANK:]], axis=1)
    fresh = fresh.astype(jnp.bfloat16)
    q = jnp.concatenate([p[:32, :] for p in (p0, p1, p2, p3)], axis=0)
    cache = cache_ref[...]
    s1 = lax.dot_general(q, cache, NT, preferred_element_type=jnp.float32)
    s2 = lax.dot_general(q, fresh, NT, preferred_element_type=jnp.float32)
    j = lax.broadcasted_iota(jnp.int32, (128, 256), 1)
    s1 = jnp.where(j < lengths[lax.axis_index("x")], s1, -1e30)
    step = (lax.broadcasted_iota(jnp.int32, (128, 8), 0) >> 3) & 3
    s2 = jnp.where(lax.broadcasted_iota(jnp.int32, (128, 8), 1) <= step, s2, -1e30)
    top = jnp.maximum(jnp.max(s1, axis=1, keepdims=True), jnp.max(s2, axis=1, keepdims=True))
    c = SCALE * LOG2E
    p_c = jnp.exp2((s1 - top) * c)
    p_n = jnp.exp2((s2 - top) * c)
    total = jnp.sum(p_c, axis=1, keepdims=True) + jnp.sum(p_n, axis=1, keepdims=True)
    acc = jnp.dot(p_c.astype(jnp.bfloat16), cache[:, :KV_RANK], preferred_element_type=jnp.float32)
    acc = acc + jnp.dot(
        p_n.astype(jnp.bfloat16), fresh[:, :KV_RANK], preferred_element_type=jnp.float32
    )
    mixed = (acc / total).astype(jnp.bfloat16)
    for k in range(4):
        out_ref[(lax.axis_index("x") + (4 - k)) & 3] = mixed[k * 32 : (k + 1) * 32]


def finish_kernel(m_ref, wuv_ref, out_ref):
    m = m_ref[...].reshape(128, KV_RANK).astype(jnp.float32)
    head = head_rows(128)
    acc = jnp.zeros((128, 128), jnp.float32)
    for h in range(8):
        mine = jnp.where(head == h, m, 0.0).astype(jnp.bfloat16)
        acc = acc + jnp.dot(mine, wuv_ref[h], preferred_element_type=jnp.float32)
    for r in range(4):
        for s in range(4):
            at = (r * 4 + s) * 8
            out_ref[s, r] = acc[at : at + 8].astype(jnp.bfloat16)


def shift(v, axis, k, n):
    return lax.ppermute(v, axis, [(i, (i + k) % n) for i in range(n)])


def copies(v, n):
    return jnp.broadcast_to(v[None], (n,) + v.shape)


def body(
    prompt_latent,
    prefill_query,
    span_start,
    w_uk,
    w_uv,
    decode_latent,
    owner_slot,
    lengths,
    hidden_new,
    decode_query,
    w_down,
    kv_gain,
):
    heads_here = w_uk.shape[0]
    queries = prefill_query.shape[0]
    width = prompt_latent.shape[1]
    bf = jnp.bfloat16
    fence = lax.optimization_barrier
    keys = lax.all_to_all(copies(prompt_latent, 8), "z", 0, 0, tiled=True)

    by_head = jnp.transpose(prefill_query, (1, 0, 2))
    rope = by_head[:, :, NOPE:]
    packed = jnp.concatenate(
        [by_head[:, :, :NOPE], jnp.concatenate([rope[:, :32], rope[:, 32:]], axis=2)], axis=1
    )
    visiting = [packed] + [shift(packed, "yh", k, 4) for k in (1, 2, 3)]
    tile = jax.ShapeDtypeStruct((40, width), bf)
    sent = small(
        prep_kernel,
        [tile] * 4,
        [decode_query, w_uk, hidden_new, w_down.T],
        0,
        [pltpu.VMEM((160, width), jnp.float32)],
        name="prep",
    )
    got = [sent[0]] + [shift(sent[k], "x", k, 4) for k in (1, 2, 3)]
    raw_here = got[0][32:].astype(jnp.float32)
    for k in (1, 2, 3):
        raw_here = raw_here + got[k][32:].astype(jnp.float32)
    rows = small(
        pack_kernel,
        jax.ShapeDtypeStruct((256, width), bf),
        [owner_slot.reshape(1, 256), jnp.transpose(decode_latent, (1, 2, 0))],
        name="pack",
    ).reshape(64, 4, width)

    keys, raw_here, rows, *rest = fence((keys, raw_here, rows, *visiting[1:]))
    visiting = [packed] + rest
    raw_there = shift(raw_here, "yl", 1, 2)
    other_keys = shift(keys, "c", 1, 2)
    cache = lax.all_to_all(rows, CTX, 0, 0, tiled=True)

    parts = small(
        flash_kernel,
        [jax.ShapeDtypeStruct((512 + 16, 128), bf)] * 4,
        [span_start, *visiting, keys, other_keys, w_uk, w_uv],
        1,
        limit=24,
        flops=4 * 2 * 512 * 1536 * 1100,
        name="flash",
    )
    parts = list(parts)
    cache, *parts = fence((cache, *parts))
    parts = [parts[0]] + [shift(parts[k], "yh", 4 - k, 4) for k in (1, 2, 3)]

    mixed = small(
        attend_kernel,
        jax.ShapeDtypeStruct((4, 32, KV_RANK), bf),
        [
            lengths,
            *got,
            raw_here,
            raw_there,
            cache.reshape(256, width),
            kv_gain.reshape(1, KV_RANK),
        ],
        1,
        limit=60,
        name="attend",
    )
    mixed = lax.all_to_all(mixed, "x", 0, 0, tiled=True)
    decode_out = small(
        finish_kernel,
        jax.ShapeDtypeStruct((4, 4, 8, 128), bf),
        [mixed, w_uv],
        name="finish",
    )
    prefill_out = merge(parts).reshape(queries, heads_here, 128)
    return (prefill_out, decode_out)


def solution(mesh):
    fine = Mesh(mesh.devices.reshape(8, 4, 2, 4, 2), ("z", "yh", "c", "x", "yl"))
    in_specs = (
        P(CTX, None),
        P(CTX, HEAD, None),
        P(),
        P(HEAD, None, None),
        P(HEAD, None, None),
        P(None, CTX, None),
        P(),
        P(CTX),
        P(None, CTX, HEAD),
        P(None, CTX, HEAD, None),
        P(HEAD, None),
        P(),
    )
    out_specs = (P(CTX, HEAD, None), P(None, CTX, HEAD, None))
    return jax.shard_map(body, mesh=fine, in_specs=in_specs, out_specs=out_specs, check_vma=False)
```

```python
import functools

import jax
import jax.numpy as jnp
from jax import lax
from jax.experimental import pallas as pl
from jax.experimental.pallas import tpu as pltpu
from jax.sharding import Mesh
from jax.sharding import PartitionSpec as P


KV_RANK = 512
ROPE = 64
NOPE = 128
LOG2E = 1.4426950408889634
SCALE = (NOPE + ROPE) ** (-0.5)
CTX = ("z", "yh", "c")
HEAD = ("x", "yl")


def split3(v):
    hi = v.astype(jnp.bfloat16)
    rest = v - hi.astype(jnp.float32)
    mid = rest.astype(jnp.bfloat16)
    low = (rest - mid.astype(jnp.float32)).astype(jnp.bfloat16)
    return hi, mid, low


def flash_kernel(offsets, start, *refs):
    count = len(offsets)
    queries, outs = dict(zip(offsets, refs[:count])), dict(zip(offsets, refs[count + 4 :]))
    k1_ref, k2_ref, wuk_ref, wuv_ref = refs[count : count + 4]
    z, yh, c = lax.axis_index("z"), lax.axis_index("yh"), lax.axis_index("c")
    k1 = k1_ref[...].reshape(768, 576)
    k2 = k2_ref[...].reshape(768, 576)
    j = lax.broadcasted_iota(jnp.int32, (1, 768), 1)
    blk = (j * 683) >> 16
    kpos = blk * 768 + (j - blk * 96) + yh * 192
    where1, where2 = kpos + c * 96, kpos + (1 - c) * 96
    scale = SCALE * LOG2E

    def score(k):
        rows = []
        for h in range(8):
            pair = queries[k][h, 64:, :]
            rope = jnp.concatenate([pair[:, :64], pair[:, 64:]], axis=0)
            a = jnp.dot(queries[k][h, :64, :], wuk_ref[h], preferred_element_type=jnp.float32)
            rows.append(jnp.concatenate([a.astype(jnp.bfloat16), rope], axis=1))
        full = jnp.concatenate(rows, axis=0)
        s1 = lax.dot_general(full, k1, NT, preferred_element_type=jnp.float32)
        s2 = lax.dot_general(full, k2, NT, preferred_element_type=jnp.float32)
        return s1, s2

    def weigh(k, s):
        source = (yh + (4 - k)) & 3
        first = start[0] + ((z * 4 + source) * 2 + c) * 64
        qpos = first + (lax.broadcasted_iota(jnp.int32, (512, 1), 0) & 63)
        s1 = jnp.where(where1 <= qpos, s[0], -1e30)
        s2 = jnp.where(where2 <= qpos, s[1], -1e30)
        top = jnp.maximum(jnp.max(s1, axis=1, keepdims=True), jnp.max(s2, axis=1, keepdims=True))
        p1 = jnp.exp2((s1 - top) * scale)
        p2 = jnp.exp2((s2 - top) * scale)
        total = jnp.sum(p1, axis=1, keepdims=True) + jnp.sum(p2, axis=1, keepdims=True)
        lse = top * scale + jnp.log2(total)
        return p1.astype(jnp.bfloat16), p2.astype(jnp.bfloat16), total, lse

    def mix(k, p1, p2, total, lse):
        acc = jnp.dot(p1, k1[:, :KV_RANK], preferred_element_type=jnp.float32)
        acc = acc + jnp.dot(p2, k2[:, :KV_RANK], preferred_element_type=jnp.float32)
        mixed = (acc / total).astype(jnp.bfloat16)
        for h in range(8):
            at = h * 64
            o = jnp.dot(mixed[at : at + 64], wuv_ref[h], preferred_element_type=jnp.float32)
            outs[k][at : at + 64, :] = o.astype(jnp.bfloat16)
        flat = jnp.transpose(jnp.broadcast_to(lse, (512, 128)))[0:1, :]
        lines = jnp.concatenate([flat[:, i * 128 : (i + 1) * 128] for i in range(4)], axis=0)
        hi, mid, low = split3(lines)
        outs[k][512:, :] = jnp.concatenate([hi, mid, low, jnp.zeros_like(hi)], axis=0)

    s = score(offsets[0])
    for n, k in enumerate(offsets):
        following = score(offsets[n + 1]) if n + 1 < count else None
        mix(k, *weigh(k, s))
        s = following


def merge_kernel(a_ref, b_ref, c_ref, d_ref, out_ref):
    parts = [a_ref, b_ref, c_ref, d_ref]
    weights = []
    for ref in parts:
        tail = ref[512:, :].astype(jnp.float32)
        weights.append(tail[0:4] + tail[4:8] + tail[8:12])
    top = jnp.maximum(jnp.maximum(weights[0], weights[1]), jnp.maximum(weights[2], weights[3]))
    weights = [jnp.exp2(w - top) for w in weights]
    inv = 1.0 / (weights[0] + weights[1] + weights[2] + weights[3])
    weights = [w * inv for w in weights]
    merged = []
    for i in range(4):
        total = jnp.zeros((128, 128), jnp.float32)
        for w, ref in zip(weights, parts):
            col = jnp.transpose(jnp.broadcast_to(w[i : i + 1, :], (128, 128)))
            total = total + col * ref[i * 128 : (i + 1) * 128, :].astype(jnp.float32)
        merged.append(total.astype(jnp.bfloat16))
    by_head = jnp.concatenate(merged, axis=0)
    row = lax.broadcasted_iota(jnp.int32, (512, 512), 0)
    col = lax.broadcasted_iota(jnp.int32, (512, 512), 1)
    pick = jnp.where(((row & 7) * 64 + (row >> 3)) == col, 1.0, 0.0).astype(jnp.bfloat16)
    out_ref[...] = jnp.dot(pick, by_head, preferred_element_type=jnp.float32).astype(jnp.bfloat16)


def small(kernel, outs, ins, scalars=0, scratch=(), limit=10, flops=1 << 27):
    vm = pl.BlockSpec(memory_space=pltpu.VMEM)
    sm = pl.BlockSpec(memory_space=pltpu.SMEM)
    return pl.pallas_call(
        kernel,
        out_shape=outs,
        in_specs=[sm] * scalars + [vm] * (len(ins) - scalars),
        out_specs=jax.tree.map(lambda _: vm, outs),
        scratch_shapes=scratch,
        compiler_params=pltpu.CompilerParams(vmem_limit_bytes=limit << 20),
        cost_estimate=pl.CostEstimate(flops=flops, bytes_accessed=1 << 20, transcendentals=1 << 12),
    )(*ins)


def merge(parts):
    return small(merge_kernel, jax.ShapeDtypeStruct((512, 128), jnp.bfloat16), parts)


NT = (((1,), (1,)), ((), ()))


def head_rows(count):
    return lax.broadcasted_iota(jnp.int32, (count, 1), 0) & 7


def prep_kernel(q_ref, wuk_ref, hid_ref, wd_ref, *refs):
    outs, rows = refs[:4], refs[4]
    q = q_ref[...].reshape(128, NOPE + ROPE)
    nope = q[:, :NOPE].astype(jnp.float32)
    head = head_rows(128)
    acc = jnp.zeros((128, KV_RANK), jnp.float32)
    for h in range(8):
        mine = jnp.where(head == h, nope, 0.0).astype(jnp.bfloat16)
        acc = acc + jnp.dot(mine, wuk_ref[h], preferred_element_type=jnp.float32)
    rows[:128, :KV_RANK] = acc
    rows[:128, KV_RANK:] = q[:, NOPE:].astype(jnp.float32)
    hidden = jnp.concatenate([hid_ref[t].astype(jnp.float32) for t in range(4)], axis=0)
    raw = lax.dot_general(
        hidden.astype(jnp.bfloat16), wd_ref[...], NT, preferred_element_type=jnp.float32
    ).astype(jnp.bfloat16)
    o = lax.broadcasted_iota(jnp.int32, (32, 16), 0)
    n = lax.broadcasted_iota(jnp.int32, (32, 16), 1)
    pick = jnp.where(((o & 7) * 4 + (o >> 3) == n) & ((o & 7) < 4), 1.0, 0.0)
    rows[128:, :] = jnp.dot(pick.astype(jnp.bfloat16), raw, preferred_element_type=jnp.float32)
    for k in range(4):
        r = (lax.axis_index("x") + k) & 3
        for s in range(4):
            at = pl.multiple_of((s * 4 + r) * 8, 8)
            outs[k][s * 8 : s * 8 + 8, :] = rows[pl.ds(at, 8), :].astype(jnp.bfloat16)
        at = pl.multiple_of(128 + r * 8, 8)
        outs[k][32:40, :] = rows[pl.ds(at, 8), :].astype(jnp.bfloat16)


def pack_kernel(owner_ref, x_ref, out_ref):
    row = lax.broadcasted_iota(jnp.int32, (512, 256), 0)
    hit = owner_ref[...] == ((row >> 3) * 4 + lax.axis_index("x"))
    acc = jnp.zeros((512, KV_RANK + ROPE), jnp.float32)
    for j in range(4):
        pick = jnp.where(hit & ((row & 7) == j), 1.0, 0.0).astype(jnp.bfloat16)
        acc = acc + lax.dot_general(pick, x_ref[j], NT, preferred_element_type=jnp.float32)
    out_ref[...] = acc.astype(jnp.bfloat16)


def spread_kernel(x_ref, out_ref):
    for i in range(8):
        out_ref[i] = x_ref[...]


def attend_kernel(lengths, p0, p1, p2, p3, raw_a, raw_b, cache_ref, gain_ref, out_ref):
    raw = raw_a[...] + raw_b[...]
    front = raw[:, :KV_RANK]
    factor = lax.rsqrt(jnp.mean(front * front, axis=1, keepdims=True) + 1e-06)
    fresh = jnp.concatenate([front * factor * gain_ref[...], raw[:, KV_RANK:]], axis=1)
    fresh = fresh.astype(jnp.bfloat16)
    q = jnp.concatenate([p[:32, :] for p in (p0, p1, p2, p3)], axis=0)
    cache = cache_ref[...]
    s1 = lax.dot_general(q, cache, NT, preferred_element_type=jnp.float32)
    s2 = lax.dot_general(q, fresh, NT, preferred_element_type=jnp.float32)
    j = lax.broadcasted_iota(jnp.int32, (128, 512), 1)
    held = ((j & 7) < 4) & ((j >> 3) * 4 + (j & 7) < lengths[lax.axis_index("x")])
    s1 = jnp.where(held, s1, -1e30)
    step = (lax.broadcasted_iota(jnp.int32, (128, 8), 0) >> 3) & 3
    s2 = jnp.where(lax.broadcasted_iota(jnp.int32, (128, 8), 1) <= step, s2, -1e30)
    top = jnp.maximum(jnp.max(s1, axis=1, keepdims=True), jnp.max(s2, axis=1, keepdims=True))
    c = SCALE * LOG2E
    p_c = jnp.exp2((s1 - top) * c)
    p_n = jnp.exp2((s2 - top) * c)
    total = jnp.sum(p_c, axis=1, keepdims=True) + jnp.sum(p_n, axis=1, keepdims=True)
    acc = jnp.dot(p_c.astype(jnp.bfloat16), cache[:, :KV_RANK], preferred_element_type=jnp.float32)
    acc = acc + jnp.dot(
        p_n.astype(jnp.bfloat16), fresh[:, :KV_RANK], preferred_element_type=jnp.float32
    )
    mixed = (acc / total).astype(jnp.bfloat16)
    for k in range(4):
        out_ref[(lax.axis_index("x") + (4 - k)) & 3] = mixed[k * 32 : (k + 1) * 32]


def finish_kernel(m_ref, wuv_ref, out_ref):
    m = m_ref[...].reshape(128, KV_RANK).astype(jnp.float32)
    head = head_rows(128)
    acc = jnp.zeros((128, 128), jnp.float32)
    for h in range(8):
        mine = jnp.where(head == h, m, 0.0).astype(jnp.bfloat16)
        acc = acc + jnp.dot(mine, wuv_ref[h], preferred_element_type=jnp.float32)
    for r in range(4):
        for s in range(4):
            at = (r * 4 + s) * 8
            out_ref[s, r] = acc[at : at + 8].astype(jnp.bfloat16)


def shift(v, axis, k, n):
    return lax.ppermute(v, axis, [(i, (i + k) % n) for i in range(n)])


def layer(
    prompt_latent,
    prefill_query,
    span_start,
    w_uk,
    w_uv,
    decode_latent,
    owner_slot,
    lengths,
    hidden_new,
    decode_query,
    w_down,
    kv_gain,
):
    heads_here = w_uk.shape[0]
    queries = prefill_query.shape[0]
    width = prompt_latent.shape[1]
    bf = jnp.bfloat16
    fence = lax.optimization_barrier
    spread = small(spread_kernel, jax.ShapeDtypeStruct((8, 96, width), bf), [prompt_latent])
    keys = lax.all_to_all(spread, "z", 0, 0, tiled=True)

    by_head = jnp.transpose(prefill_query, (1, 0, 2))
    rope = by_head[:, :, NOPE:]
    packed = jnp.concatenate(
        [by_head[:, :, :NOPE], jnp.concatenate([rope[:, :32], rope[:, 32:]], axis=2)], axis=1
    )
    visiting = [packed] + [None] * 3
    for k in (2, 1, 3):
        visiting[k] = shift(packed, "yh", k, 4)
    tile = jax.ShapeDtypeStruct((40, width), bf)
    sent = small(
        prep_kernel,
        [tile] * 4,
        [decode_query, w_uk, hidden_new, w_down.T],
        0,
        [pltpu.VMEM((160, width), jnp.float32)],
    )
    got = [sent[0]] + [None] * 3
    for k in (2, 1, 3):
        got[k] = shift(sent[k], "x", k, 4)
    raw_here = got[0][32:].astype(jnp.float32)
    for k in (1, 2, 3):
        raw_here = raw_here + got[k][32:].astype(jnp.float32)
    rows = small(
        pack_kernel,
        jax.ShapeDtypeStruct((512, width), bf),
        [owner_slot.reshape(1, 256), jnp.transpose(decode_latent, (1, 2, 0))],
    ).reshape(64, 8, width)

    keys, raw_here, rows, *rest = fence((keys, raw_here, rows, *visiting[1:]))
    visiting = [packed] + rest
    raw_there = shift(raw_here, "yl", 1, 2)
    other_keys = shift(keys, "c", 1, 2)
    cache = lax.all_to_all(rows, CTX, 0, 0, tiled=True)

    def flash(offsets, chunks):
        return small(
            functools.partial(flash_kernel, offsets),
            [jax.ShapeDtypeStruct((512 + 16, 128), bf)] * len(offsets),
            [span_start, *chunks, keys, other_keys, w_uk, w_uv],
            1,
            limit=24,
            flops=len(offsets) * 2 * 512 * 1536 * 1100,
        )

    far = (2, 1, 3)
    sending = flash(far, [visiting[k] for k in far])
    cache, *sending = fence((cache, *sending))
    parts = [None] * 4
    for k, piece in zip(far, sending):
        parts[k] = shift(piece, "yh", 4 - k, 4)

    mixed = small(
        attend_kernel,
        jax.ShapeDtypeStruct((4, 32, KV_RANK), bf),
        [
            lengths,
            *got,
            raw_here,
            raw_there,
            cache.reshape(512, width),
            kv_gain.reshape(1, KV_RANK),
        ],
        1,
        limit=16,
    )
    own, mixed = fence((packed, mixed))
    mixed = lax.all_to_all(mixed, "x", 0, 0, tiled=True)
    parts[0] = flash((0,), [own])[0]
    mixed, parts[0] = fence((mixed, parts[0]))
    decode_out = small(finish_kernel, jax.ShapeDtypeStruct((4, 4, 8, 128), bf), [mixed, w_uv])
    prefill_out = merge(parts).reshape(queries, heads_here, 128)
    return (prefill_out, decode_out)


def solution(mesh):
    fine = Mesh(mesh.devices.reshape(8, 4, 2, 4, 2), ("z", "yh", "c", "x", "yl"))
    in_specs = (
        P(CTX, None),
        P(CTX, HEAD, None),
        P(),
        P(HEAD, None, None),
        P(HEAD, None, None),
        P(None, CTX, None),
        P(),
        P(CTX),
        P(None, CTX, HEAD),
        P(None, CTX, HEAD, None),
        P(HEAD, None),
        P(),
    )
    out_specs = (P(CTX, HEAD, None), P(None, CTX, HEAD, None))
    return jax.shard_map(layer, mesh=fine, in_specs=in_specs, out_specs=out_specs, check_vma=False)
```

```python
import functools

import jax
import jax.numpy as jnp
from jax import lax
from jax.experimental import pallas as pl
from jax.experimental.pallas import tpu as pltpu
from jax.sharding import Mesh
from jax.sharding import PartitionSpec as P


KV_RANK = 512
ROPE = 64
NOPE = 128
LOG2E = 1.4426950408889634
SCALE = (NOPE + ROPE) ** (-0.5)
CTX = ("z", "yh", "c")
HEAD = ("x", "yl")


def split3(v):
    hi = v.astype(jnp.bfloat16)
    rest = v - hi.astype(jnp.float32)
    mid = rest.astype(jnp.bfloat16)
    low = (rest - mid.astype(jnp.float32)).astype(jnp.bfloat16)
    return hi, mid, low


def flash_kernel(offsets, start, *refs):
    count = len(offsets)
    moved, (wuk_ref, wuv_ref), targets = refs[: count + 2], refs[count + 2 : count + 4], refs[count + 4 : 2 * count + 4]
    held, out_held, sems = refs[2 * count + 4 : 3 * count + 6], refs[3 * count + 6 : -1], refs[-1]
    loads = [pltpu.make_async_copy(m, h, sems.at[i]) for i, (m, h) in enumerate(zip(moved, held))]
    for load in loads:
        load.start()
    queries, outs = dict(zip(offsets, held[:count])), dict(zip(offsets, out_held))
    k1_ref, k2_ref = held[count:]
    stores = []
    z, yh, c = lax.axis_index("z"), lax.axis_index("yh"), lax.axis_index("c")
    for load in loads:
        load.wait()
    k1 = k1_ref[...].reshape(768, 576)
    k2 = k2_ref[...].reshape(768, 576)
    j = lax.broadcasted_iota(jnp.int32, (1, 768), 1)
    blk = (j * 683) >> 16
    kpos = blk * 768 + (j - blk * 96) + yh * 192
    where1, where2 = kpos + c * 96, kpos + (1 - c) * 96
    scale = SCALE * LOG2E

    def score(k):
        rows = []
        for h in range(8):
            pair = queries[k][h, 64:, :]
            rope = jnp.concatenate([pair[:, :64], pair[:, 64:]], axis=0)
            a = jnp.dot(queries[k][h, :64, :], wuk_ref[h], preferred_element_type=jnp.float32)
            rows.append(jnp.concatenate([a.astype(jnp.bfloat16), rope], axis=1))
        full = jnp.concatenate(rows, axis=0)
        s1 = lax.dot_general(full, k1, NT, preferred_element_type=jnp.float32)
        s2 = lax.dot_general(full, k2, NT, preferred_element_type=jnp.float32)
        return s1, s2

    def weigh(k, s):
        source = (yh + (4 - k)) & 3
        first = start[0] + ((z * 4 + source) * 2 + c) * 64
        qpos = first + (lax.broadcasted_iota(jnp.int32, (512, 1), 0) & 63)
        s1 = jnp.where(where1 <= qpos, s[0], -1e30)
        s2 = jnp.where(where2 <= qpos, s[1], -1e30)
        top = jnp.maximum(jnp.max(s1, axis=1, keepdims=True), jnp.max(s2, axis=1, keepdims=True))
        p1 = jnp.exp2((s1 - top) * scale)
        p2 = jnp.exp2((s2 - top) * scale)
        total = jnp.sum(p1, axis=1, keepdims=True) + jnp.sum(p2, axis=1, keepdims=True)
        lse = top * scale + jnp.log2(total)
        return p1.astype(jnp.bfloat16), p2.astype(jnp.bfloat16), total, lse

    def mix(k, p1, p2, total, lse):
        acc = jnp.dot(p1, k1[:, :KV_RANK], preferred_element_type=jnp.float32)
        acc = acc + jnp.dot(p2, k2[:, :KV_RANK], preferred_element_type=jnp.float32)
        mixed = (acc * (1.0 / total)).astype(jnp.bfloat16)
        for h in range(8):
            at = h * 64
            o = jnp.dot(mixed[at : at + 64], wuv_ref[h], preferred_element_type=jnp.float32)
            outs[k][at : at + 64, :] = o.astype(jnp.bfloat16)
        flat = jnp.transpose(jnp.broadcast_to(lse, (512, 128)))[0:1, :]
        lines = jnp.concatenate([flat[:, i * 128 : (i + 1) * 128] for i in range(4)], axis=0)
        hi, mid, low = split3(lines)
        outs[k][512:, :] = jnp.concatenate([hi, mid, low, jnp.zeros_like(hi)], axis=0)

    s = score(offsets[0])
    for n, k in enumerate(offsets):
        following = score(offsets[n + 1]) if n + 1 < count else None
        mix(k, *weigh(k, s))
        store = pltpu.make_async_copy(outs[k], targets[n], sems.at[count + 2 + n])
        store.start()
        stores.append(store)
        s = following
    for store in stores:
        store.wait()


def merge_kernel(a_ref, b_ref, c_ref, d_ref, out_ref):
    parts = [a_ref, b_ref, c_ref, d_ref]
    weights = []
    for ref in parts:
        tail = ref[512:, :].astype(jnp.float32)
        weights.append(tail[0:4] + tail[4:8] + tail[8:12])
    top = jnp.maximum(jnp.maximum(weights[0], weights[1]), jnp.maximum(weights[2], weights[3]))
    weights = [jnp.exp2(w - top) for w in weights]
    inv = 1.0 / (weights[0] + weights[1] + weights[2] + weights[3])
    weights = [w * inv for w in weights]
    merged = []
    for i in range(4):
        total = jnp.zeros((128, 128), jnp.float32)
        for w, ref in zip(weights, parts):
            col = jnp.transpose(jnp.broadcast_to(w[i : i + 1, :], (128, 128)))
            total = total + col * ref[i * 128 : (i + 1) * 128, :].astype(jnp.float32)
        merged.append(total.astype(jnp.bfloat16))
    by_head = jnp.concatenate(merged, axis=0)
    row = lax.broadcasted_iota(jnp.int32, (512, 512), 0)
    col = lax.broadcasted_iota(jnp.int32, (512, 512), 1)
    pick = jnp.where(((row & 7) * 64 + (row >> 3)) == col, 1.0, 0.0).astype(jnp.bfloat16)
    out_ref[...] = jnp.dot(pick, by_head, preferred_element_type=jnp.float32).astype(jnp.bfloat16)


def small(kernel, outs, ins, scalars=0, scratch=(), limit=10, flops=1 << 27):
    vm = pl.BlockSpec(memory_space=pltpu.VMEM)
    sm = pl.BlockSpec(memory_space=pltpu.SMEM)
    return pl.pallas_call(
        kernel,
        out_shape=outs,
        in_specs=[sm] * scalars + [vm] * (len(ins) - scalars),
        out_specs=jax.tree.map(lambda _: vm, outs),
        scratch_shapes=scratch,
        compiler_params=pltpu.CompilerParams(vmem_limit_bytes=limit << 20),
        cost_estimate=pl.CostEstimate(flops=flops, bytes_accessed=1 << 20, transcendentals=1 << 12),
    )(*ins)


def merge(parts):
    return small(merge_kernel, jax.ShapeDtypeStruct((512, 128), jnp.bfloat16), parts)


NT = (((1,), (1,)), ((), ()))


def head_rows(count):
    return lax.broadcasted_iota(jnp.int32, (count, 1), 0) & 7


def prep_kernel(q_ref, wuk_ref, hid_ref, wd_ref, *refs):
    outs, rows = refs[:4], refs[4]
    q = q_ref[...].reshape(128, NOPE + ROPE)
    nope = q[:, :NOPE].astype(jnp.float32)
    head = head_rows(128)
    acc = jnp.zeros((128, KV_RANK), jnp.float32)
    for h in range(8):
        mine = jnp.where(head == h, nope, 0.0).astype(jnp.bfloat16)
        acc = acc + jnp.dot(mine, wuk_ref[h], preferred_element_type=jnp.float32)
    rows[:128, :KV_RANK] = acc
    rows[:128, KV_RANK:] = q[:, NOPE:].astype(jnp.float32)
    hidden = jnp.concatenate([hid_ref[t].astype(jnp.float32) for t in range(4)], axis=0)
    raw = lax.dot_general(
        hidden.astype(jnp.bfloat16), wd_ref[...], NT, preferred_element_type=jnp.float32
    ).astype(jnp.bfloat16)
    o = lax.broadcasted_iota(jnp.int32, (32, 16), 0)
    n = lax.broadcasted_iota(jnp.int32, (32, 16), 1)
    pick = jnp.where(((o & 7) * 4 + (o >> 3) == n) & ((o & 7) < 4), 1.0, 0.0)
    rows[128:, :] = jnp.dot(pick.astype(jnp.bfloat16), raw, preferred_element_type=jnp.float32)
    for k in range(4):
        r = (lax.axis_index("x") + k) & 3
        for s in range(4):
            at = pl.multiple_of((s * 4 + r) * 8, 8)
            outs[k][s * 8 : s * 8 + 8, :] = rows[pl.ds(at, 8), :].astype(jnp.bfloat16)
        at = pl.multiple_of(128 + r * 8, 8)
        outs[k][32:40, :] = rows[pl.ds(at, 8), :].astype(jnp.bfloat16)


def pack_kernel(owner_ref, x_ref, out_ref):
    row = lax.broadcasted_iota(jnp.int32, (512, 256), 0)
    hit = owner_ref[...] == ((row >> 3) * 4 + lax.axis_index("x"))
    acc = jnp.zeros((512, KV_RANK + ROPE), jnp.float32)
    for j in range(4):
        pick = jnp.where(hit & ((row & 7) == j), 1.0, 0.0).astype(jnp.bfloat16)
        acc = acc + lax.dot_general(pick, x_ref[j], NT, preferred_element_type=jnp.float32)
    out_ref[...] = acc.astype(jnp.bfloat16)


def spread_kernel(x_ref, out_ref, held, sems):
    take = pltpu.make_async_copy(x_ref, held, sems.at[8])
    take.start()
    take.wait()
    moves = [pltpu.make_async_copy(held, out_ref.at[i], sems.at[i]) for i in range(8)]
    for move in moves:
        move.start()
    for move in moves:
        move.wait()


def attend_kernel(lengths, p0, p1, p2, p3, raw_a, raw_b, cache_ref, gain_ref, out_ref):
    raw = raw_a[...] + raw_b[...]
    front = raw[:, :KV_RANK]
    factor = lax.rsqrt(jnp.mean(front * front, axis=1, keepdims=True) + 1e-06)
    fresh = jnp.concatenate([front * factor * gain_ref[...], raw[:, KV_RANK:]], axis=1)
    fresh = fresh.astype(jnp.bfloat16)
    q = jnp.concatenate([p[:32, :] for p in (p0, p1, p2, p3)], axis=0)
    cache = cache_ref[...]
    s1 = lax.dot_general(q, cache, NT, preferred_element_type=jnp.float32)
    s2 = lax.dot_general(q, fresh, NT, preferred_element_type=jnp.float32)
    j = lax.broadcasted_iota(jnp.int32, (128, 512), 1)
    held = ((j & 7) < 4) & ((j >> 3) * 4 + (j & 7) < lengths[lax.axis_index("x")])
    s1 = jnp.where(held, s1, -1e30)
    step = (lax.broadcasted_iota(jnp.int32, (128, 8), 0) >> 3) & 3
    s2 = jnp.where(lax.broadcasted_iota(jnp.int32, (128, 8), 1) <= step, s2, -1e30)
    top = jnp.maximum(jnp.max(s1, axis=1, keepdims=True), jnp.max(s2, axis=1, keepdims=True))
    c = SCALE * LOG2E
    p_c = jnp.exp2((s1 - top) * c)
    p_n = jnp.exp2((s2 - top) * c)
    total = jnp.sum(p_c, axis=1, keepdims=True) + jnp.sum(p_n, axis=1, keepdims=True)
    acc = jnp.dot(p_c.astype(jnp.bfloat16), cache[:, :KV_RANK], preferred_element_type=jnp.float32)
    acc = acc + jnp.dot(
        p_n.astype(jnp.bfloat16), fresh[:, :KV_RANK], preferred_element_type=jnp.float32
    )
    mixed = (acc / total).astype(jnp.bfloat16)
    for k in range(4):
        out_ref[(lax.axis_index("x") + (4 - k)) & 3] = mixed[k * 32 : (k + 1) * 32]


def finish_kernel(m_ref, wuv_ref, out_ref):
    m = m_ref[...].reshape(128, KV_RANK).astype(jnp.float32)
    head = head_rows(128)
    acc = jnp.zeros((128, 128), jnp.float32)
    for h in range(8):
        mine = jnp.where(head == h, m, 0.0).astype(jnp.bfloat16)
        acc = acc + jnp.dot(mine, wuv_ref[h], preferred_element_type=jnp.float32)
    for r in range(4):
        for s in range(4):
            at = (r * 4 + s) * 8
            out_ref[s, r] = acc[at : at + 8].astype(jnp.bfloat16)


def shift(v, axis, k, n):
    return lax.ppermute(v, axis, [(i, (i + k) % n) for i in range(n)])


def layer(
    prompt_latent,
    prefill_query,
    span_start,
    w_uk,
    w_uv,
    decode_latent,
    owner_slot,
    lengths,
    hidden_new,
    decode_query,
    w_down,
    kv_gain,
):
    heads_here = w_uk.shape[0]
    queries = prefill_query.shape[0]
    width = prompt_latent.shape[1]
    bf = jnp.bfloat16
    fence = lax.optimization_barrier
    hbm = pl.BlockSpec(memory_space=pltpu.HBM)
    spread = pl.pallas_call(
        spread_kernel,
        out_shape=jax.ShapeDtypeStruct((8, 96, width), bf),
        in_specs=[hbm],
        out_specs=hbm,
        scratch_shapes=[pltpu.VMEM((96, width), bf), pltpu.SemaphoreType.DMA((9,))],
        compiler_params=pltpu.CompilerParams(vmem_limit_bytes=4 << 20),
        cost_estimate=pl.CostEstimate(flops=1 << 10, bytes_accessed=1 << 20, transcendentals=0),
        name="spread",
    )(prompt_latent)
    keys = lax.all_to_all(spread, "z", 0, 0, tiled=True)

    by_head = jnp.transpose(prefill_query, (1, 0, 2))
    rope = by_head[:, :, NOPE:]
    packed = jnp.concatenate(
        [by_head[:, :, :NOPE], jnp.concatenate([rope[:, :32], rope[:, 32:]], axis=2)], axis=1
    )
    visiting = [packed] + [None] * 3
    for k in (2, 1, 3):
        visiting[k] = shift(packed, "yh", k, 4)
    tile = jax.ShapeDtypeStruct((40, width), bf)
    sent = small(
        prep_kernel,
        [tile] * 4,
        [decode_query, w_uk, hidden_new, w_down.T],
        0,
        [pltpu.VMEM((160, width), jnp.float32)],
    )
    got = [sent[0]] + [None] * 3
    for k in (2, 1, 3):
        got[k] = shift(sent[k], "x", k, 4)
    raw_here = got[0][32:].astype(jnp.float32)
    for k in (1, 2, 3):
        raw_here = raw_here + got[k][32:].astype(jnp.float32)
    rows = small(
        pack_kernel,
        jax.ShapeDtypeStruct((512, width), bf),
        [owner_slot.reshape(1, 256), jnp.transpose(decode_latent, (1, 2, 0))],
    ).reshape(64, 8, width)

    keys, raw_here, rows = fence((keys, raw_here, rows))
    raw_there = shift(raw_here, "yl", 1, 2)
    other_keys = shift(keys, "c", 1, 2)
    cache = lax.all_to_all(rows, CTX, 0, 0, tiled=True)

    def flash(offsets, chunks):
        count = len(offsets)
        chunk, key = pltpu.VMEM((8, 96, 128), bf), pltpu.VMEM((8, 96, width), bf)
        vmem = pl.BlockSpec(memory_space=pltpu.VMEM)
        return pl.pallas_call(
            functools.partial(flash_kernel, offsets),
            out_shape=[jax.ShapeDtypeStruct((512 + 16, 128), bf)] * count,
            in_specs=[pl.BlockSpec(memory_space=pltpu.SMEM)] + [hbm] * (count + 2) + [vmem] * 2,
            out_specs=[hbm] * count,
            scratch_shapes=[chunk] * count
            + [key] * 2
            + [pltpu.VMEM((512 + 16, 128), bf)] * count
            + [pltpu.SemaphoreType.DMA((2 * count + 2,))],
            compiler_params=pltpu.CompilerParams(vmem_limit_bytes=28 << 20),
            cost_estimate=pl.CostEstimate(
                flops=count * 2 * 512 * 1536 * 1100, bytes_accessed=4 << 20, transcendentals=1 << 20
            ),
            name="flash",
        )(span_start, *chunks, keys, other_keys, w_uk, w_uv)

    far = (2, 1, 3)
    sending = flash(far, [visiting[k] for k in far])
    parts = [None] * 4
    for k, piece in zip(far, sending):
        parts[k] = shift(piece, "yh", 4 - k, 4)

    mixed = small(
        attend_kernel,
        jax.ShapeDtypeStruct((4, 32, KV_RANK), bf),
        [
            lengths,
            *got,
            raw_here,
            raw_there,
            cache.reshape(512, width),
            kv_gain.reshape(1, KV_RANK),
        ],
        1,
        limit=10,
    )
    own, mixed = fence((packed, mixed))
    mixed = lax.all_to_all(mixed, "x", 0, 0, tiled=True)
    parts[0] = flash((0,), [own])[0]
    mixed, parts[0] = fence((mixed, parts[0]))
    decode_out = small(finish_kernel, jax.ShapeDtypeStruct((4, 4, 8, 128), bf), [mixed, w_uv])
    prefill_out = merge(parts).reshape(queries, heads_here, 128)
    return (prefill_out, decode_out)


def solution(mesh):
    fine = Mesh(mesh.devices.reshape(8, 4, 2, 4, 2), ("z", "yh", "c", "x", "yl"))
    in_specs = (
        P(CTX, None),
        P(CTX, HEAD, None),
        P(),
        P(HEAD, None, None),
        P(HEAD, None, None),
        P(None, CTX, None),
        P(),
        P(CTX),
        P(None, CTX, HEAD),
        P(None, CTX, HEAD, None),
        P(HEAD, None),
        P(),
    )
    out_specs = (P(CTX, HEAD, None), P(None, CTX, HEAD, None))
    return jax.shard_map(layer, mesh=fine, in_specs=in_specs, out_specs=out_specs, check_vma=False)
```

```python
import functools

import jax
import jax.numpy as jnp
from jax import lax
from jax.experimental import pallas as pl
from jax.experimental.pallas import tpu as pltpu
from jax.sharding import Mesh
from jax.sharding import PartitionSpec as P


KV_RANK = 512
ROPE = 64
NOPE = 128
LOG2E = 1.4426950408889634
SCALE = (NOPE + ROPE) ** (-0.5)
CTX = ("z", "yh", "c")
HEAD = ("x", "yl")


def split3(v):
    hi = v.astype(jnp.bfloat16)
    rest = v - hi.astype(jnp.float32)
    mid = rest.astype(jnp.bfloat16)
    low = (rest - mid.astype(jnp.float32)).astype(jnp.bfloat16)
    return hi, mid, low


def flash_kernel(offsets, start, *refs):
    count = len(offsets)
    moved, (wuk_ref, wuv_ref), targets = refs[: count + 2], refs[count + 2 : count + 4], refs[count + 4 : 2 * count + 4]
    held, out_held, sems = refs[2 * count + 4 : 3 * count + 6], refs[3 * count + 6 : -1], refs[-1]
    loads = [pltpu.make_async_copy(m, h, sems.at[i]) for i, (m, h) in enumerate(zip(moved, held))]
    for load in (loads[0], *loads[count:], *loads[1:count]):
        load.start()
    queries, outs = dict(zip(offsets, held[:count])), dict(zip(offsets, out_held))
    k1_ref, k2_ref = held[count:]
    stores = []
    z, yh, c = lax.axis_index("z"), lax.axis_index("yh"), lax.axis_index("c")
    waits = dict(zip((*offsets, "k1", "k2"), loads))
    ready = {}

    def key_rows(name, ref):
        if name not in ready:
            waits[name].wait()
            ready[name] = ref[...].reshape(768, 576)
        return ready[name]

    j = lax.broadcasted_iota(jnp.int32, (1, 768), 1)
    blk = (j * 683) >> 16
    kpos = blk * 768 + (j - blk * 96) + yh * 192
    where1, where2 = kpos + c * 96, kpos + (1 - c) * 96
    scale = SCALE * LOG2E

    def score(k):
        rows = []
        waits[k].wait()
        for h in range(8):
            pair = queries[k][h, 64:, :]
            rope = jnp.concatenate([pair[:, :64], pair[:, 64:]], axis=0)
            a = jnp.dot(queries[k][h, :64, :], wuk_ref[h], preferred_element_type=jnp.float32)
            rows.append(jnp.concatenate([a.astype(jnp.bfloat16), rope], axis=1))
        full = jnp.concatenate(rows, axis=0)
        s1 = lax.dot_general(full, key_rows("k1", k1_ref), NT, preferred_element_type=jnp.float32)
        s2 = lax.dot_general(full, key_rows("k2", k2_ref), NT, preferred_element_type=jnp.float32)
        return s1, s2

    def weigh(k, s):
        source = (yh + (4 - k)) & 3
        first = start[0] + ((z * 4 + source) * 2 + c) * 64
        qpos = first + (lax.broadcasted_iota(jnp.int32, (512, 1), 0) & 63)
        s1 = jnp.where(where1 <= qpos, s[0], -1e30)
        s2 = jnp.where(where2 <= qpos, s[1], -1e30)
        top = jnp.maximum(jnp.max(s1, axis=1, keepdims=True), jnp.max(s2, axis=1, keepdims=True))
        p1 = jnp.exp2((s1 - top) * scale)
        p2 = jnp.exp2((s2 - top) * scale)
        total = jnp.sum(p1, axis=1, keepdims=True) + jnp.sum(p2, axis=1, keepdims=True)
        lse = top * scale + jnp.log2(total)
        return p1.astype(jnp.bfloat16), p2.astype(jnp.bfloat16), total, lse

    def mix(k, p1, p2, total, lse):
        acc = jnp.dot(p1, ready["k1"][:, :KV_RANK], preferred_element_type=jnp.float32)
        acc = acc + jnp.dot(p2, ready["k2"][:, :KV_RANK], preferred_element_type=jnp.float32)
        mixed = (acc * (1.0 / total)).astype(jnp.bfloat16)
        for h in range(8):
            at = h * 64
            o = jnp.dot(mixed[at : at + 64], wuv_ref[h], preferred_element_type=jnp.float32)
            outs[k][at : at + 64, :] = o.astype(jnp.bfloat16)
        flat = jnp.transpose(jnp.broadcast_to(lse, (512, 128)))[0:1, :]
        lines = jnp.concatenate([flat[:, i * 128 : (i + 1) * 128] for i in range(4)], axis=0)
        hi, mid, low = split3(lines)
        outs[k][512:, :] = jnp.concatenate([hi, mid, low, jnp.zeros_like(hi)], axis=0)

    s = score(offsets[0])
    for n, k in enumerate(offsets):
        following = score(offsets[n + 1]) if n + 1 < count else None
        mix(k, *weigh(k, s))
        store = pltpu.make_async_copy(outs[k], targets[n], sems.at[count + 2 + n])
        store.start()
        stores.append(store)
        s = following
    for store in stores:
        store.wait()


def merge_kernel(a_ref, b_ref, c_ref, d_ref, out_ref):
    parts = [a_ref, b_ref, c_ref, d_ref]
    weights = []
    for ref in parts:
        tail = ref[512:, :].astype(jnp.float32)
        weights.append(tail[0:4] + tail[4:8] + tail[8:12])
    top = jnp.maximum(jnp.maximum(weights[0], weights[1]), jnp.maximum(weights[2], weights[3]))
    weights = [jnp.exp2(w - top) for w in weights]
    inv = 1.0 / (weights[0] + weights[1] + weights[2] + weights[3])
    weights = [w * inv for w in weights]
    merged = []
    for i in range(4):
        total = jnp.zeros((128, 128), jnp.float32)
        for w, ref in zip(weights, parts):
            col = jnp.transpose(jnp.broadcast_to(w[i : i + 1, :], (128, 128)))
            total = total + col * ref[i * 128 : (i + 1) * 128, :].astype(jnp.float32)
        merged.append(total.astype(jnp.bfloat16))
    by_head = jnp.concatenate(merged, axis=0)
    row = lax.broadcasted_iota(jnp.int32, (512, 512), 0)
    col = lax.broadcasted_iota(jnp.int32, (512, 512), 1)
    pick = jnp.where(((row & 7) * 64 + (row >> 3)) == col, 1.0, 0.0).astype(jnp.bfloat16)
    out_ref[...] = jnp.dot(pick, by_head, preferred_element_type=jnp.float32).astype(jnp.bfloat16)


def small(kernel, outs, ins, scalars=0, scratch=(), limit=10, flops=1 << 27):
    vm = pl.BlockSpec(memory_space=pltpu.VMEM)
    sm = pl.BlockSpec(memory_space=pltpu.SMEM)
    return pl.pallas_call(
        kernel,
        out_shape=outs,
        in_specs=[sm] * scalars + [vm] * (len(ins) - scalars),
        out_specs=jax.tree.map(lambda _: vm, outs),
        scratch_shapes=scratch,
        compiler_params=pltpu.CompilerParams(vmem_limit_bytes=limit << 20),
        cost_estimate=pl.CostEstimate(flops=flops, bytes_accessed=1 << 20, transcendentals=1 << 12),
    )(*ins)


def merge(parts):
    return small(merge_kernel, jax.ShapeDtypeStruct((512, 128), jnp.bfloat16), parts)


NT = (((1,), (1,)), ((), ()))


def head_rows(count):
    return lax.broadcasted_iota(jnp.int32, (count, 1), 0) & 7


def prep_kernel(q_ref, wuk_ref, hid_ref, wd_ref, *refs):
    near, next_, far, rows = refs
    outs = (near, next_, far.at[:40], far.at[40:])
    q = q_ref[...].reshape(128, NOPE + ROPE)
    nope = q[:, :NOPE].astype(jnp.float32)
    head = head_rows(128)
    acc = jnp.zeros((128, KV_RANK), jnp.float32)
    for h in range(8):
        mine = jnp.where(head == h, nope, 0.0).astype(jnp.bfloat16)
        acc = acc + jnp.dot(mine, wuk_ref[h], preferred_element_type=jnp.float32)
    rows[:128, :KV_RANK] = acc
    rows[:128, KV_RANK:] = q[:, NOPE:].astype(jnp.float32)
    hidden = jnp.concatenate([hid_ref[t].astype(jnp.float32) for t in range(4)], axis=0)
    raw = lax.dot_general(
        hidden.astype(jnp.bfloat16), wd_ref[...], NT, preferred_element_type=jnp.float32
    ).astype(jnp.bfloat16)
    o = lax.broadcasted_iota(jnp.int32, (32, 16), 0)
    n = lax.broadcasted_iota(jnp.int32, (32, 16), 1)
    pick = jnp.where(((o & 7) * 4 + (o >> 3) == n) & ((o & 7) < 4), 1.0, 0.0)
    rows[128:, :] = jnp.dot(pick.astype(jnp.bfloat16), raw, preferred_element_type=jnp.float32)
    for k in range(4):
        r = lax.axis_index("x") ^ k
        for s in range(4):
            at = pl.multiple_of((s * 4 + r) * 8, 8)
            outs[k][s * 8 : s * 8 + 8, :] = rows[pl.ds(at, 8), :].astype(jnp.bfloat16)
        at = pl.multiple_of(128 + r * 8, 8)
        outs[k][32:40, :] = rows[pl.ds(at, 8), :].astype(jnp.bfloat16)


def pack_kernel(owner_ref, x_ref, out_ref):
    row = lax.broadcasted_iota(jnp.int32, (512, 256), 0)
    hit = owner_ref[...] == ((row >> 3) * 4 + lax.axis_index("x"))
    acc = jnp.zeros((512, KV_RANK + ROPE), jnp.float32)
    for j in range(4):
        pick = jnp.where(hit & ((row & 7) == j), 1.0, 0.0).astype(jnp.bfloat16)
        acc = acc + lax.dot_general(pick, x_ref[j], NT, preferred_element_type=jnp.float32)
    out_ref[...] = acc.astype(jnp.bfloat16)


def spread_kernel(x_ref, out_ref, sems):
    moves = [pltpu.make_async_copy(x_ref, out_ref.at[i], sems.at[i]) for i in range(8)]
    for move in moves:
        move.start()
    for move in moves:
        move.wait()


def attend_kernel(lengths, p0, p13, p2, raw_a, raw_b, cache_ref, gain_ref, out_ref):
    raw = raw_a[...] + raw_b[...]
    front = raw[:, :KV_RANK]
    factor = lax.rsqrt(jnp.mean(front * front, axis=1, keepdims=True) + 1e-06)
    fresh = jnp.concatenate([front * factor * gain_ref[...], raw[:, KV_RANK:]], axis=1)
    fresh = fresh.astype(jnp.bfloat16)
    q = jnp.concatenate([p0[:32], p13[:32], p2[:32], p13[40:72]], axis=0)
    cache = cache_ref[...]
    s1 = lax.dot_general(q, cache, NT, preferred_element_type=jnp.float32)
    s2 = lax.dot_general(q, fresh, NT, preferred_element_type=jnp.float32)
    j = lax.broadcasted_iota(jnp.int32, (128, 512), 1)
    held = ((j & 7) < 4) & ((j >> 3) * 4 + (j & 7) < lengths[lax.axis_index("x")])
    s1 = jnp.where(held, s1, -1e30)
    step = (lax.broadcasted_iota(jnp.int32, (128, 8), 0) >> 3) & 3
    s2 = jnp.where(lax.broadcasted_iota(jnp.int32, (128, 8), 1) <= step, s2, -1e30)
    top = jnp.maximum(jnp.max(s1, axis=1, keepdims=True), jnp.max(s2, axis=1, keepdims=True))
    c = SCALE * LOG2E
    p_c = jnp.exp2((s1 - top) * c)
    p_n = jnp.exp2((s2 - top) * c)
    total = jnp.sum(p_c, axis=1, keepdims=True) + jnp.sum(p_n, axis=1, keepdims=True)
    acc = jnp.dot(p_c.astype(jnp.bfloat16), cache[:, :KV_RANK], preferred_element_type=jnp.float32)
    acc = acc + jnp.dot(
        p_n.astype(jnp.bfloat16), fresh[:, :KV_RANK], preferred_element_type=jnp.float32
    )
    mixed = (acc / total).astype(jnp.bfloat16)
    for k in range(4):
        out_ref[lax.axis_index("x") ^ k] = mixed[k * 32 : (k + 1) * 32]


def finish_kernel(m_ref, wuv_ref, out_ref):
    m = m_ref[...].reshape(128, KV_RANK).astype(jnp.float32)
    head = head_rows(128)
    acc = jnp.zeros((128, 128), jnp.float32)
    for h in range(8):
        mine = jnp.where(head == h, m, 0.0).astype(jnp.bfloat16)
        acc = acc + jnp.dot(mine, wuv_ref[h], preferred_element_type=jnp.float32)
    for r in range(4):
        for s in range(4):
            at = (r * 4 + s) * 8
            out_ref[s, r] = acc[at : at + 8].astype(jnp.bfloat16)


def shift(v, axis, k, n):
    return lax.ppermute(v, axis, [(i, (i + k) % n) for i in range(n)])


def trade(v, axis, k, n):
    return lax.ppermute(v, axis, [(i, i ^ k) for i in range(n)])


def layer(
    prompt_latent,
    prefill_query,
    span_start,
    w_uk,
    w_uv,
    decode_latent,
    owner_slot,
    lengths,
    hidden_new,
    decode_query,
    w_down,
    kv_gain,
):
    heads_here = w_uk.shape[0]
    queries = prefill_query.shape[0]
    width = prompt_latent.shape[1]
    bf = jnp.bfloat16
    fence = lax.optimization_barrier
    hbm = pl.BlockSpec(memory_space=pltpu.HBM)
    spread = pl.pallas_call(
        spread_kernel,
        out_shape=jax.ShapeDtypeStruct((8, 96, width), bf),
        in_specs=[pl.BlockSpec(memory_space=pltpu.VMEM)],
        out_specs=hbm,
        scratch_shapes=[pltpu.SemaphoreType.DMA((8,))],
        compiler_params=pltpu.CompilerParams(vmem_limit_bytes=4 << 20),
        cost_estimate=pl.CostEstimate(flops=1 << 10, bytes_accessed=1 << 20, transcendentals=0),
        name="spread",
    )(prompt_latent)
    keys = lax.all_to_all(spread, "z", 0, 0, tiled=True)

    by_head = jnp.transpose(prefill_query, (1, 0, 2))
    rope = by_head[:, :, NOPE:]
    packed = jnp.concatenate(
        [by_head[:, :, :NOPE], jnp.concatenate([rope[:, :32], rope[:, 32:]], axis=2)], axis=1
    )
    visiting = [packed] + [None] * 3
    for k in (2, 1, 3):
        visiting[k] = shift(packed, "yh", k, 4)
    tile = jax.ShapeDtypeStruct((40, width), bf)
    near, following, far_two = small(
        prep_kernel,
        [tile, tile, jax.ShapeDtypeStruct((80, width), bf)],
        [decode_query, w_uk, hidden_new, w_down.T],
        0,
        [pltpu.VMEM((160, width), jnp.float32)],
    )
    from_two = trade(far_two, "x", 2, 4)
    relay = jnp.concatenate([following, from_two[40:]], axis=0)
    from_one = trade(relay, "x", 1, 4)
    got = (near, from_one, from_two)
    raw_here = near[32:].astype(jnp.float32) + from_two[32:40].astype(jnp.float32)
    raw_here = raw_here + from_one[32:40].astype(jnp.float32) + from_one[72:].astype(jnp.float32)
    raw_there = trade(raw_here, "yl", 1, 2)
    rows = small(
        pack_kernel,
        jax.ShapeDtypeStruct((512, width), bf),
        [owner_slot.reshape(1, 256), jnp.transpose(decode_latent, (1, 2, 0))],
    ).reshape(64, 8, width)

    keys, rows = fence((keys, rows))
    other_keys = shift(keys, "c", 1, 2)
    cache = lax.all_to_all(rows, CTX, 0, 0, tiled=True)

    def flash(offsets, chunks):
        count = len(offsets)
        chunk, key = pltpu.VMEM((8, 96, 128), bf), pltpu.VMEM((8, 96, width), bf)
        vmem = pl.BlockSpec(memory_space=pltpu.VMEM)
        return pl.pallas_call(
            functools.partial(flash_kernel, offsets),
            out_shape=[jax.ShapeDtypeStruct((512 + 16, 128), bf)] * count,
            in_specs=[pl.BlockSpec(memory_space=pltpu.SMEM)] + [hbm] * (count + 2) + [vmem] * 2,
            out_specs=[hbm] * count,
            scratch_shapes=[chunk] * count
            + [key] * 2
            + [pltpu.VMEM((512 + 16, 128), bf)] * count
            + [pltpu.SemaphoreType.DMA((2 * count + 2,))],
            compiler_params=pltpu.CompilerParams(vmem_limit_bytes=28 << 20),
            cost_estimate=pl.CostEstimate(
                flops=count * 2 * 512 * 1536 * 1100, bytes_accessed=4 << 20, transcendentals=1 << 20
            ),
            name="flash",
        )(span_start, *chunks, keys, other_keys, w_uk, w_uv)

    far = (2, 1, 3)
    sending = flash(far, [visiting[k] for k in far])
    parts = [None] * 4
    for k, piece in zip(far, sending):
        parts[k] = shift(piece, "yh", 4 - k, 4)

    mixed = small(
        attend_kernel,
        jax.ShapeDtypeStruct((4, 32, KV_RANK), bf),
        [
            lengths,
            *got,
            raw_here,
            raw_there,
            cache.reshape(512, width),
            kv_gain.reshape(1, KV_RANK),
        ],
        1,
        limit=60,
    )
    own, mixed = fence((packed, mixed))
    mixed = lax.all_to_all(mixed, "x", 0, 0, tiled=True)
    parts[0] = flash((0,), [own])[0]
    mixed, parts[0] = fence((mixed, parts[0]))
    decode_out = small(finish_kernel, jax.ShapeDtypeStruct((4, 4, 8, 128), bf), [mixed, w_uv])
    prefill_out = merge(parts).reshape(queries, heads_here, 128)
    return (prefill_out, decode_out)


def solution(mesh):
    fine = Mesh(mesh.devices.reshape(8, 4, 2, 4, 2), ("z", "yh", "c", "x", "yl"))
    in_specs = (
        P(CTX, None),
        P(CTX, HEAD, None),
        P(),
        P(HEAD, None, None),
        P(HEAD, None, None),
        P(None, CTX, None),
        P(),
        P(CTX),
        P(None, CTX, HEAD),
        P(None, CTX, HEAD, None),
        P(HEAD, None),
        P(),
    )
    out_specs = (P(CTX, HEAD, None), P(None, CTX, HEAD, None))
    return jax.shard_map(layer, mesh=fine, in_specs=in_specs, out_specs=out_specs, check_vma=False)
```

```python
import functools

import jax
import jax.numpy as jnp
from jax import lax
from jax.experimental import pallas as pl
from jax.experimental.pallas import tpu as pltpu
from jax.sharding import Mesh
from jax.sharding import PartitionSpec as P


KV_RANK = 512
ROPE = 64
NOPE = 128
LOG2E = 1.4426950408889634
SCALE = (NOPE + ROPE) ** (-0.5)
CTX = ("z", "yh", "c")
HEAD = ("x", "yl")


def split3(v):
    hi = v.astype(jnp.bfloat16)
    rest = v - hi.astype(jnp.float32)
    mid = rest.astype(jnp.bfloat16)
    low = (rest - mid.astype(jnp.float32)).astype(jnp.bfloat16)
    return hi, mid, low


def flash_kernel(offsets, start, *refs):
    count = len(offsets)
    moved, targets = refs[: count + 4], refs[count + 4 : 2 * count + 4]
    held, out_held, sems = refs[2 * count + 4 : 3 * count + 8], refs[3 * count + 8 : -1], refs[-1]
    loads = [pltpu.make_async_copy(m, h, sems.at[i]) for i, (m, h) in enumerate(zip(moved, held))]
    for at in (0, count + 2, count, count + 1, *range(1, count), count + 3):
        loads[at].start()
    queries, outs = dict(zip(offsets, held[:count])), dict(zip(offsets, out_held))
    k1_ref, k2_ref, wuk_ref, wuv_ref = held[count:]
    stores = []
    z, yh, c = lax.axis_index("z"), lax.axis_index("yh"), lax.axis_index("c")
    waits = dict(zip((*offsets, "k1", "k2", "wuk", "wuv"), loads))
    ready = {}

    def key_rows(name, ref):
        if name not in ready:
            waits[name].wait()
            ready[name] = ref[...].reshape(768, 576)
        return ready[name]

    j = lax.broadcasted_iota(jnp.int32, (1, 768), 1)
    blk = (j * 683) >> 16
    kpos = blk * 768 + (j - blk * 96) + yh * 192
    where1, where2 = kpos + c * 96, kpos + (1 - c) * 96
    scale = SCALE * LOG2E

    def score(k):
        rows = []
        waits[k].wait()
        if k == offsets[0]:
            waits["wuk"].wait()
        for h in range(8):
            pair = queries[k][h, 64:, :]
            rope = jnp.concatenate([pair[:, :64], pair[:, 64:]], axis=0)
            a = jnp.dot(queries[k][h, :64, :], wuk_ref[h], preferred_element_type=jnp.float32)
            rows.append(jnp.concatenate([a.astype(jnp.bfloat16), rope], axis=1))
        full = jnp.concatenate(rows, axis=0)
        s1 = lax.dot_general(full, key_rows("k1", k1_ref), NT, preferred_element_type=jnp.float32)
        s2 = lax.dot_general(full, key_rows("k2", k2_ref), NT, preferred_element_type=jnp.float32)
        return s1, s2

    def weigh(k, s):
        source = yh ^ k
        first = start[0] + ((z * 4 + source) * 2 + c) * 64
        qpos = first + (lax.broadcasted_iota(jnp.int32, (512, 1), 0) & 63)
        s1 = jnp.where(where1 <= qpos, s[0], -1e30)
        s2 = jnp.where(where2 <= qpos, s[1], -1e30)
        top = jnp.maximum(jnp.max(s1, axis=1, keepdims=True), jnp.max(s2, axis=1, keepdims=True))
        p1 = jnp.exp2((s1 - top) * scale)
        p2 = jnp.exp2((s2 - top) * scale)
        total = jnp.sum(p1, axis=1, keepdims=True) + jnp.sum(p2, axis=1, keepdims=True)
        lse = top * scale + jnp.log2(total)
        return p1.astype(jnp.bfloat16), p2.astype(jnp.bfloat16), total, lse

    def mix(k, p1, p2, total, lse):
        if k == offsets[0]:
            waits["wuv"].wait()
        acc = jnp.dot(p1, ready["k1"][:, :KV_RANK], preferred_element_type=jnp.float32)
        acc = acc + jnp.dot(p2, ready["k2"][:, :KV_RANK], preferred_element_type=jnp.float32)
        mixed = (acc * (1.0 / total)).astype(jnp.bfloat16)
        for h in range(8):
            at = h * 64
            o = jnp.dot(mixed[at : at + 64], wuv_ref[h], preferred_element_type=jnp.float32)
            outs[k][at : at + 64, :] = o.astype(jnp.bfloat16)
        flat = jnp.transpose(jnp.broadcast_to(lse, (512, 128)))[0:1, :]
        lines = jnp.concatenate([flat[:, i * 128 : (i + 1) * 128] for i in range(4)], axis=0)
        hi, mid, low = split3(lines)
        outs[k][512:, :] = jnp.concatenate([hi, mid, low, jnp.zeros_like(hi)], axis=0)

    s = score(offsets[0])
    for n, k in enumerate(offsets):
        following = score(offsets[n + 1]) if n + 1 < count else None
        mix(k, *weigh(k, s))
        store = pltpu.make_async_copy(outs[k], targets[n], sems.at[count + 4 + n])
        store.start()
        stores.append(store)
        s = following
    for store in stores:
        store.wait()


def merge_kernel(a_ref, b_ref, c_ref, d_ref, out_ref):
    parts = [a_ref, b_ref, c_ref, d_ref]
    weights = []
    for ref in parts:
        tail = ref[512:, :].astype(jnp.float32)
        weights.append(tail[0:4] + tail[4:8] + tail[8:12])
    top = jnp.maximum(jnp.maximum(weights[0], weights[1]), jnp.maximum(weights[2], weights[3]))
    weights = [jnp.exp2(w - top) for w in weights]
    inv = 1.0 / (weights[0] + weights[1] + weights[2] + weights[3])
    weights = [w * inv for w in weights]
    merged = []
    for i in range(4):
        total = jnp.zeros((128, 128), jnp.float32)
        for w, ref in zip(weights, parts):
            col = jnp.transpose(jnp.broadcast_to(w[i : i + 1, :], (128, 128)))
            total = total + col * ref[i * 128 : (i + 1) * 128, :].astype(jnp.float32)
        merged.append(total.astype(jnp.bfloat16))
    by_head = jnp.concatenate(merged, axis=0)
    row = lax.broadcasted_iota(jnp.int32, (512, 512), 0)
    col = lax.broadcasted_iota(jnp.int32, (512, 512), 1)
    pick = jnp.where(((row & 7) * 64 + (row >> 3)) == col, 1.0, 0.0).astype(jnp.bfloat16)
    out_ref[...] = jnp.dot(pick, by_head, preferred_element_type=jnp.float32).astype(jnp.bfloat16)


def small(kernel, outs, ins, scalars=0, scratch=(), limit=10, flops=1 << 27):
    vm = pl.BlockSpec(memory_space=pltpu.VMEM)
    sm = pl.BlockSpec(memory_space=pltpu.SMEM)
    return pl.pallas_call(
        kernel,
        out_shape=outs,
        in_specs=[sm] * scalars + [vm] * (len(ins) - scalars),
        out_specs=jax.tree.map(lambda _: vm, outs),
        scratch_shapes=scratch,
        compiler_params=pltpu.CompilerParams(vmem_limit_bytes=limit << 20),
        cost_estimate=pl.CostEstimate(flops=flops, bytes_accessed=1 << 20, transcendentals=1 << 12),
    )(*ins)


def merge(parts):
    return small(merge_kernel, jax.ShapeDtypeStruct((512, 128), jnp.bfloat16), parts)


NT = (((1,), (1,)), ((), ()))


def head_rows(count):
    return lax.broadcasted_iota(jnp.int32, (count, 1), 0) & 7


def prep_kernel(q_ref, wuk_ref, hid_ref, wd_ref, *refs):
    near, next_, far, rows = refs
    outs = (near, next_, far.at[:40], far.at[40:])
    q = q_ref[...].reshape(128, NOPE + ROPE)
    nope = q[:, :NOPE].astype(jnp.float32)
    head = head_rows(128)
    acc = jnp.zeros((128, KV_RANK), jnp.float32)
    for h in range(8):
        mine = jnp.where(head == h, nope, 0.0).astype(jnp.bfloat16)
        acc = acc + jnp.dot(mine, wuk_ref[h], preferred_element_type=jnp.float32)
    rows[:128, :KV_RANK] = acc
    rows[:128, KV_RANK:] = q[:, NOPE:].astype(jnp.float32)
    hidden = jnp.concatenate([hid_ref[t].astype(jnp.float32) for t in range(4)], axis=0)
    raw = lax.dot_general(
        hidden.astype(jnp.bfloat16), wd_ref[...], NT, preferred_element_type=jnp.float32
    ).astype(jnp.bfloat16)
    o = lax.broadcasted_iota(jnp.int32, (32, 16), 0)
    n = lax.broadcasted_iota(jnp.int32, (32, 16), 1)
    pick = jnp.where(((o & 7) * 4 + (o >> 3) == n) & ((o & 7) < 4), 1.0, 0.0)
    rows[128:, :] = jnp.dot(pick.astype(jnp.bfloat16), raw, preferred_element_type=jnp.float32)
    for k in range(4):
        r = lax.axis_index("x") ^ k
        for s in range(4):
            at = pl.multiple_of((s * 4 + r) * 8, 8)
            outs[k][s * 8 : s * 8 + 8, :] = rows[pl.ds(at, 8), :].astype(jnp.bfloat16)
        at = pl.multiple_of(128 + r * 8, 8)
        outs[k][32:40, :] = rows[pl.ds(at, 8), :].astype(jnp.bfloat16)


def pack_kernel(owner_ref, x_ref, out_ref):
    row = lax.broadcasted_iota(jnp.int32, (512, 256), 0)
    hit = owner_ref[...] == ((row >> 3) * 4 + lax.axis_index("x"))
    acc = jnp.zeros((512, KV_RANK + ROPE), jnp.float32)
    for j in range(4):
        pick = jnp.where(hit & ((row & 7) == j), 1.0, 0.0).astype(jnp.bfloat16)
        acc = acc + lax.dot_general(pick, x_ref[j], NT, preferred_element_type=jnp.float32)
    out_ref[...] = acc.astype(jnp.bfloat16)


def spread_kernel(x_ref, out_ref, sems):
    moves = [pltpu.make_async_copy(x_ref, out_ref.at[i], sems.at[i]) for i in range(8)]
    for move in moves:
        move.start()
    for move in moves:
        move.wait()


def attend_kernel(p0, p13, p2, raw_a, raw_b, cache_ref, out_ref):
    lane = lax.broadcasted_iota(jnp.int32, (1, KV_RANK + ROPE), 1)
    length = jnp.where(lane == lax.axis_index("x"), raw_a[6:7, :], 0.0)
    length = jnp.sum(length, axis=1, keepdims=True).astype(jnp.int32)
    raw = raw_a[...] + raw_b[...]
    front = raw[:, :KV_RANK]
    factor = lax.rsqrt(jnp.mean(front * front, axis=1, keepdims=True) + 1e-06)
    fresh = jnp.concatenate([front * factor * raw_a[5:6, :KV_RANK], raw[:, KV_RANK:]], axis=1)
    fresh = fresh.astype(jnp.bfloat16)
    q = jnp.concatenate([p0[:32], p13[:32], p2[:32], p13[40:72]], axis=0)
    cache = cache_ref[...]
    s1 = lax.dot_general(q, cache, NT, preferred_element_type=jnp.float32)
    s2 = lax.dot_general(q, fresh, NT, preferred_element_type=jnp.float32)
    j = lax.broadcasted_iota(jnp.int32, (128, 512), 1)
    held = ((j & 7) < 4) & ((j >> 3) * 4 + (j & 7) < length)
    s1 = jnp.where(held, s1, -1e30)
    step = (lax.broadcasted_iota(jnp.int32, (128, 8), 0) >> 3) & 3
    s2 = jnp.where(lax.broadcasted_iota(jnp.int32, (128, 8), 1) <= step, s2, -1e30)
    top = jnp.maximum(jnp.max(s1, axis=1, keepdims=True), jnp.max(s2, axis=1, keepdims=True))
    c = SCALE * LOG2E
    p_c = jnp.exp2((s1 - top) * c)
    p_n = jnp.exp2((s2 - top) * c)
    total = jnp.sum(p_c, axis=1, keepdims=True) + jnp.sum(p_n, axis=1, keepdims=True)
    acc = jnp.dot(p_c.astype(jnp.bfloat16), cache[:, :KV_RANK], preferred_element_type=jnp.float32)
    acc = acc + jnp.dot(
        p_n.astype(jnp.bfloat16), fresh[:, :KV_RANK], preferred_element_type=jnp.float32
    )
    mixed = (acc / total).astype(jnp.bfloat16)
    for k in range(4):
        out_ref[lax.axis_index("x") ^ k] = mixed[k * 32 : (k + 1) * 32]


def finish_kernel(m_ref, wuv_ref, out_ref):
    m = m_ref[...].reshape(128, KV_RANK).astype(jnp.float32)
    head = head_rows(128)
    acc = jnp.zeros((128, 128), jnp.float32)
    for h in range(8):
        mine = jnp.where(head == h, m, 0.0).astype(jnp.bfloat16)
        acc = acc + jnp.dot(mine, wuv_ref[h], preferred_element_type=jnp.float32)
    for r in range(4):
        for s in range(4):
            at = (r * 4 + s) * 8
            out_ref[s, r] = acc[at : at + 8].astype(jnp.bfloat16)


def trade(v, axis, k, n):
    return lax.ppermute(v, axis, [(i, i ^ k) for i in range(n)])


def layer(
    prompt_latent,
    prefill_query,
    span_start,
    w_uk,
    w_uv,
    decode_latent,
    owner_slot,
    lengths,
    hidden_new,
    decode_query,
    w_down,
    kv_gain,
):
    heads_here = w_uk.shape[0]
    queries = prefill_query.shape[0]
    width = prompt_latent.shape[1]
    bf = jnp.bfloat16
    fence = lax.optimization_barrier
    hbm = pl.BlockSpec(memory_space=pltpu.HBM)
    spread = pl.pallas_call(
        spread_kernel,
        out_shape=jax.ShapeDtypeStruct((8, 96, width), bf),
        in_specs=[pl.BlockSpec(memory_space=pltpu.VMEM)],
        out_specs=hbm,
        scratch_shapes=[pltpu.SemaphoreType.DMA((8,))],
        compiler_params=pltpu.CompilerParams(vmem_limit_bytes=4 << 20),
        cost_estimate=pl.CostEstimate(flops=1 << 10, bytes_accessed=1 << 20, transcendentals=0),
        name="spread",
    )(prompt_latent)
    keys = lax.all_to_all(spread, "z", 0, 0, tiled=True)

    by_head = jnp.transpose(prefill_query, (1, 0, 2))
    rope = by_head[:, :, NOPE:]
    packed = jnp.concatenate(
        [by_head[:, :, :NOPE], jnp.concatenate([rope[:, :32], rope[:, 32:]], axis=2)], axis=1
    )
    visiting = [packed] + [None] * 3
    for k in (2, 1, 3):
        visiting[k] = trade(packed, "yh", k, 4)
    tile = jax.ShapeDtypeStruct((40, width), bf)
    near, following, far_two = small(
        prep_kernel,
        [tile, tile, jax.ShapeDtypeStruct((80, width), bf)],
        [decode_query, w_uk, hidden_new, w_down.T],
        0,
        [pltpu.VMEM((160, width), jnp.float32)],
    )
    from_two = trade(far_two, "x", 2, 4)
    relay = jnp.concatenate([following, from_two[40:]], axis=0)
    from_one = trade(relay, "x", 1, 4)
    got = (near, from_one, from_two)
    raw_here = near[32:].astype(jnp.float32) + from_two[32:40].astype(jnp.float32)
    raw_here = raw_here + from_one[32:40].astype(jnp.float32) + from_one[72:].astype(jnp.float32)
    raw_here = raw_here + jnp.pad(kv_gain[None], ((5, 2), (0, width - KV_RANK)))
    raw_here = raw_here + jnp.pad(lengths.astype(jnp.float32)[None], ((6, 1), (0, width - 4)))
    raw_there = trade(raw_here, "yl", 1, 2)
    rows = small(
        pack_kernel,
        jax.ShapeDtypeStruct((512, width), bf),
        [owner_slot.reshape(1, 256), jnp.transpose(decode_latent, (1, 2, 0))],
    ).reshape(64, 8, width)

    keys, rows = fence((keys, rows))
    other_keys = trade(keys, "c", 1, 2)
    cache = lax.all_to_all(rows, CTX, 0, 0, tiled=True)

    def flash(offsets, chunks):
        count = len(offsets)
        chunk, key = pltpu.VMEM((8, 96, 128), bf), pltpu.VMEM((8, 96, width), bf)
        return pl.pallas_call(
            functools.partial(flash_kernel, offsets),
            out_shape=[jax.ShapeDtypeStruct((512 + 16, 128), bf)] * count,
            in_specs=[pl.BlockSpec(memory_space=pltpu.SMEM)] + [hbm] * (count + 4),
            out_specs=[hbm] * count,
            scratch_shapes=[chunk] * count
            + [key] * 2
            + [pltpu.VMEM(w_uk.shape, bf), pltpu.VMEM(w_uv.shape, bf)]
            + [pltpu.VMEM((512 + 16, 128), bf)] * count
            + [pltpu.SemaphoreType.DMA((2 * count + 4,))],
            compiler_params=pltpu.CompilerParams(vmem_limit_bytes=28 << 20),
            cost_estimate=pl.CostEstimate(
                flops=count * 2 * 512 * 1536 * 1100, bytes_accessed=4 << 20, transcendentals=1 << 20
            ),
            name="flash",
        )(span_start, *chunks, keys, other_keys, w_uk, w_uv)

    far = (2, 1, 3)
    sending = flash(far, [visiting[k] for k in far])
    parts = [None] * 4
    for k, piece in zip(far, sending):
        parts[k] = trade(piece, "yh", k, 4)

    mixed = small(
        attend_kernel,
        jax.ShapeDtypeStruct((4, 32, KV_RANK), bf),
        [*got, raw_here, raw_there, cache.reshape(512, width)],
    )
    own, mixed = fence((packed, mixed))
    mixed = lax.all_to_all(mixed, "x", 0, 0, tiled=True)
    parts[0] = flash((0,), [own])[0]
    mixed, parts[0] = fence((mixed, parts[0]))
    decode_out = small(finish_kernel, jax.ShapeDtypeStruct((4, 4, 8, 128), bf), [mixed, w_uv])
    prefill_out = merge(parts).reshape(queries, heads_here, 128)
    return (prefill_out, decode_out)


def solution(mesh):
    fine = Mesh(mesh.devices.reshape(8, 4, 2, 4, 2), ("z", "yh", "c", "x", "yl"))
    in_specs = (
        P(CTX, None),
        P(CTX, HEAD, None),
        P(),
        P(HEAD, None, None),
        P(HEAD, None, None),
        P(None, CTX, None),
        P(),
        P(CTX),
        P(None, CTX, HEAD),
        P(None, CTX, HEAD, None),
        P(HEAD, None),
        P(),
    )
    out_specs = (P(CTX, HEAD, None), P(None, CTX, HEAD, None))
    return jax.shard_map(layer, mesh=fine, in_specs=in_specs, out_specs=out_specs, check_vma=False)
```

```python
import jax
import jax.numpy as jnp
from jax import lax
from jax.experimental import pallas as pl
from jax.experimental.pallas import tpu as pltpu
from jax.sharding import Mesh
from jax.sharding import PartitionSpec as P


KV_RANK = 512
ROPE = 64
NOPE = 128
LOG2E = 1.4426950408889634
SCALE = (NOPE + ROPE) ** (-0.5)
CTX = ("z", "yh", "c")
HEAD = ("x", "yl")


def split3(v):
    hi = v.astype(jnp.bfloat16)
    rest = v - hi.astype(jnp.float32)
    mid = rest.astype(jnp.bfloat16)
    low = (rest - mid.astype(jnp.float32)).astype(jnp.bfloat16)
    return hi, mid, low


def flash_kernel(start, q0, q1, q2, q3, k1_hbm, k2_hbm, wuk_ref, wuv_ref, *refs):
    targets, held, outs, sems = refs[:4], refs[4:10], refs[10:14], refs[14]
    loads = [
        pltpu.make_async_copy(m, h, sems.at[i])
        for i, (m, h) in enumerate(zip((q0, q1, q2, q3, k1_hbm, k2_hbm), held))
    ]
    for load in loads:
        load.start()
    queries, k1_ref, k2_ref = held[:4], held[4], held[5]
    z, yh, c = lax.axis_index("z"), lax.axis_index("yh"), lax.axis_index("c")
    j = lax.broadcasted_iota(jnp.int32, (1, 768), 1)
    blk = (j * 683) >> 16
    kpos = blk * 768 + (j - blk * 96) + yh * 192
    where1, where2 = kpos + c * 96, kpos + (1 - c) * 96
    row = lax.broadcasted_iota(jnp.int32, (512, 1), 0)
    source = ((row >> 6) & 3) ^ yh
    qpos = start[0] + ((source + z * 4) * 2 + c) * 64 + (row & 63)
    scale = SCALE * LOG2E
    keys = []
    lines = [[], [], [], []]

    def score(b):
        rows = []
        for h in (2 * b, 2 * b + 1):
            nope = jnp.concatenate([q[h, :64, :] for q in queries], axis=0)
            a = jnp.dot(nope, wuk_ref[h], preferred_element_type=jnp.float32)
            ropes = []
            for q in queries:
                pair = q[h, 64:, :]
                ropes += [pair[:, :64], pair[:, 64:]]
            rope = jnp.concatenate(ropes, axis=0)
            rows.append(jnp.concatenate([a.astype(jnp.bfloat16), rope], axis=1))
        full = jnp.concatenate(rows, axis=0)
        if not keys:
            for load, ref in ((loads[4], k1_ref), (loads[5], k2_ref)):
                load.wait()
                keys.append(ref[...].reshape(768, 576))
        return [lax.dot_general(full, k, NT, preferred_element_type=jnp.float32) for k in keys]

    def weigh(s):
        s1 = jnp.where(where1 <= qpos, s[0], -1e30)
        s2 = jnp.where(where2 <= qpos, s[1], -1e30)
        top = jnp.maximum(jnp.max(s1, axis=1, keepdims=True), jnp.max(s2, axis=1, keepdims=True))
        p1 = jnp.exp2((s1 - top) * scale)
        p2 = jnp.exp2((s2 - top) * scale)
        total = jnp.sum(p1, axis=1, keepdims=True) + jnp.sum(p2, axis=1, keepdims=True)
        lse = top * scale + jnp.log2(total)
        return p1.astype(jnp.bfloat16), p2.astype(jnp.bfloat16), total, lse

    def mix(b, p1, p2, total, lse):
        acc = jnp.dot(p1, keys[0][:, :KV_RANK], preferred_element_type=jnp.float32)
        acc = acc + jnp.dot(p2, keys[1][:, :KV_RANK], preferred_element_type=jnp.float32)
        mixed = (acc * (1.0 / total)).astype(jnp.bfloat16)
        for n in (0, 1):
            h = 2 * b + n
            o = jnp.dot(
                mixed[n * 256 : (n + 1) * 256], wuv_ref[h], preferred_element_type=jnp.float32
            ).astype(jnp.bfloat16)
            for k in range(4):
                outs[k][h * 64 : (h + 1) * 64, :] = o[k * 64 : (k + 1) * 64]
        flat = jnp.transpose(jnp.broadcast_to(lse, (512, 128)))[0:1, :]
        for k in range(4):
            at = k * 64
            lines[k].append(
                jnp.concatenate([flat[:, at : at + 64], flat[:, at + 256 : at + 320]], axis=1)
            )

    for load in loads[:4]:
        load.wait()
    s = score(0)
    for b in range(4):
        following = score(b + 1) if b < 3 else None
        mix(b, *weigh(s))
        s = following
    stores = []
    for k in (2, 1, 3, 0):
        hi, mid, low = split3(jnp.concatenate(lines[k], axis=0))
        outs[k][512:, :] = jnp.concatenate([hi, mid, low, jnp.zeros_like(hi)], axis=0)
        stores.append(pltpu.make_async_copy(outs[k], targets[k], sems.at[6 + k]))
        stores[-1].start()
    for store in stores:
        store.wait()


def merge_kernel(a_ref, b_ref, c_ref, d_ref, out_ref):
    parts = [a_ref, b_ref, c_ref, d_ref]
    weights = []
    for ref in parts:
        tail = ref[512:, :].astype(jnp.float32)
        weights.append(tail[0:4] + tail[4:8] + tail[8:12])
    top = jnp.maximum(jnp.maximum(weights[0], weights[1]), jnp.maximum(weights[2], weights[3]))
    weights = [jnp.exp2(w - top) for w in weights]
    inv = 1.0 / (weights[0] + weights[1] + weights[2] + weights[3])
    weights = [w * inv for w in weights]
    merged = []
    for i in range(4):
        total = jnp.zeros((128, 128), jnp.float32)
        for w, ref in zip(weights, parts):
            col = jnp.transpose(jnp.broadcast_to(w[i : i + 1, :], (128, 128)))
            total = total + col * ref[i * 128 : (i + 1) * 128, :].astype(jnp.float32)
        merged.append(total.astype(jnp.bfloat16))
    by_head = jnp.concatenate(merged, axis=0)
    row = lax.broadcasted_iota(jnp.int32, (512, 512), 0)
    col = lax.broadcasted_iota(jnp.int32, (512, 512), 1)
    pick = jnp.where(((row & 7) * 64 + (row >> 3)) == col, 1.0, 0.0).astype(jnp.bfloat16)
    out_ref[...] = jnp.dot(pick, by_head, preferred_element_type=jnp.float32).astype(jnp.bfloat16)


def small(kernel, outs, ins, scalars=0, scratch=(), limit=10, flops=1 << 27):
    vm = pl.BlockSpec(memory_space=pltpu.VMEM)
    sm = pl.BlockSpec(memory_space=pltpu.SMEM)
    return pl.pallas_call(
        kernel,
        out_shape=outs,
        in_specs=[sm] * scalars + [vm] * (len(ins) - scalars),
        out_specs=jax.tree.map(lambda _: vm, outs),
        scratch_shapes=scratch,
        compiler_params=pltpu.CompilerParams(vmem_limit_bytes=limit << 20),
        cost_estimate=pl.CostEstimate(flops=flops, bytes_accessed=1 << 20, transcendentals=1 << 12),
    )(*ins)


def merge(parts):
    return small(merge_kernel, jax.ShapeDtypeStruct((512, 128), jnp.bfloat16), parts)


NT = (((1,), (1,)), ((), ()))


def head_rows(count):
    return lax.broadcasted_iota(jnp.int32, (count, 1), 0) & 7


def prep_kernel(q_ref, wuk_ref, hid_ref, wd_ref, *refs):
    near, next_, far, rows = refs
    outs = (near, next_, far.at[:40], far.at[40:])
    q = q_ref[...].reshape(128, NOPE + ROPE)
    nope = q[:, :NOPE].astype(jnp.float32)
    head = head_rows(128)
    acc = jnp.zeros((128, KV_RANK), jnp.float32)
    for h in range(8):
        mine = jnp.where(head == h, nope, 0.0).astype(jnp.bfloat16)
        acc = acc + jnp.dot(mine, wuk_ref[h], preferred_element_type=jnp.float32)
    rows[:128, :KV_RANK] = acc
    rows[:128, KV_RANK:] = q[:, NOPE:].astype(jnp.float32)
    hidden = jnp.concatenate([hid_ref[t].astype(jnp.float32) for t in range(4)], axis=0)
    raw = lax.dot_general(
        hidden.astype(jnp.bfloat16), wd_ref[...], NT, preferred_element_type=jnp.float32
    ).astype(jnp.bfloat16)
    o = lax.broadcasted_iota(jnp.int32, (32, 16), 0)
    n = lax.broadcasted_iota(jnp.int32, (32, 16), 1)
    pick = jnp.where(((o & 7) * 4 + (o >> 3) == n) & ((o & 7) < 4), 1.0, 0.0)
    rows[128:, :] = jnp.dot(pick.astype(jnp.bfloat16), raw, preferred_element_type=jnp.float32)
    for k in range(4):
        r = lax.axis_index("x") ^ k
        for s in range(4):
            at = pl.multiple_of((s * 4 + r) * 8, 8)
            outs[k][s * 8 : s * 8 + 8, :] = rows[pl.ds(at, 8), :].astype(jnp.bfloat16)
        at = pl.multiple_of(128 + r * 8, 8)
        outs[k][32:40, :] = rows[pl.ds(at, 8), :].astype(jnp.bfloat16)


def pack_kernel(owner_ref, x_ref, out_ref):
    row = lax.broadcasted_iota(jnp.int32, (512, 256), 0)
    hit = owner_ref[...] == ((row >> 3) * 4 + lax.axis_index("x"))
    acc = jnp.zeros((512, KV_RANK + ROPE), jnp.float32)
    for j in range(4):
        pick = jnp.where(hit & ((row & 7) == j), 1.0, 0.0).astype(jnp.bfloat16)
        acc = acc + lax.dot_general(pick, x_ref[j], NT, preferred_element_type=jnp.float32)
    out_ref[...] = acc.astype(jnp.bfloat16)


def spread_kernel(x_ref, out_ref, sems):
    moves = [pltpu.make_async_copy(x_ref, out_ref.at[i], sems.at[i]) for i in range(8)]
    for move in moves:
        move.start()
    for move in moves:
        move.wait()


def attend_kernel(p0, p13, p2, raw_a, raw_b, cache_ref, out_ref):
    lane = lax.broadcasted_iota(jnp.int32, (1, KV_RANK + ROPE), 1)
    length = jnp.where(lane == lax.axis_index("x"), raw_a[6:7, :], 0.0)
    length = jnp.sum(length, axis=1, keepdims=True).astype(jnp.int32)
    raw = raw_a[...] + raw_b[...]
    front = raw[:, :KV_RANK]
    factor = lax.rsqrt(jnp.mean(front * front, axis=1, keepdims=True) + 1e-06)
    fresh = jnp.concatenate([front * factor * raw_a[5:6, :KV_RANK], raw[:, KV_RANK:]], axis=1)
    fresh = fresh.astype(jnp.bfloat16)
    q = jnp.concatenate([p0[:32], p13[:32], p2[:32], p13[40:72]], axis=0)
    cache = cache_ref[...]
    s1 = lax.dot_general(q, cache, NT, preferred_element_type=jnp.float32)
    s2 = lax.dot_general(q, fresh, NT, preferred_element_type=jnp.float32)
    j = lax.broadcasted_iota(jnp.int32, (128, 512), 1)
    held = ((j & 7) < 4) & ((j >> 3) * 4 + (j & 7) < length)
    s1 = jnp.where(held, s1, -1e30)
    step = (lax.broadcasted_iota(jnp.int32, (128, 8), 0) >> 3) & 3
    s2 = jnp.where(lax.broadcasted_iota(jnp.int32, (128, 8), 1) <= step, s2, -1e30)
    top = jnp.maximum(jnp.max(s1, axis=1, keepdims=True), jnp.max(s2, axis=1, keepdims=True))
    c = SCALE * LOG2E
    p_c = jnp.exp2((s1 - top) * c)
    p_n = jnp.exp2((s2 - top) * c)
    total = jnp.sum(p_c, axis=1, keepdims=True) + jnp.sum(p_n, axis=1, keepdims=True)
    acc = jnp.dot(p_c.astype(jnp.bfloat16), cache[:, :KV_RANK], preferred_element_type=jnp.float32)
    acc = acc + jnp.dot(
        p_n.astype(jnp.bfloat16), fresh[:, :KV_RANK], preferred_element_type=jnp.float32
    )
    mixed = (acc / total).astype(jnp.bfloat16)
    for k in range(4):
        out_ref[lax.axis_index("x") ^ k] = mixed[k * 32 : (k + 1) * 32]


def finish_kernel(m_ref, wuv_ref, out_ref):
    m = m_ref[...].reshape(128, KV_RANK).astype(jnp.float32)
    head = head_rows(128)
    acc = jnp.zeros((128, 128), jnp.float32)
    for h in range(8):
        mine = jnp.where(head == h, m, 0.0).astype(jnp.bfloat16)
        acc = acc + jnp.dot(mine, wuv_ref[h], preferred_element_type=jnp.float32)
    for r in range(4):
        for s in range(4):
            at = (r * 4 + s) * 8
            out_ref[s, r] = acc[at : at + 8].astype(jnp.bfloat16)


def trade(v, axis, k, n):
    return lax.ppermute(v, axis, [(i, i ^ k) for i in range(n)])


def layer(
    prompt_latent,
    prefill_query,
    span_start,
    w_uk,
    w_uv,
    decode_latent,
    owner_slot,
    lengths,
    hidden_new,
    decode_query,
    w_down,
    kv_gain,
):
    heads_here = w_uk.shape[0]
    queries = prefill_query.shape[0]
    width = prompt_latent.shape[1]
    bf = jnp.bfloat16
    fence = lax.optimization_barrier
    hbm = pl.BlockSpec(memory_space=pltpu.HBM)
    spread = pl.pallas_call(
        spread_kernel,
        out_shape=jax.ShapeDtypeStruct((8, 96, width), bf),
        in_specs=[pl.BlockSpec(memory_space=pltpu.VMEM)],
        out_specs=hbm,
        scratch_shapes=[pltpu.SemaphoreType.DMA((8,))],
        compiler_params=pltpu.CompilerParams(vmem_limit_bytes=4 << 20),
        cost_estimate=pl.CostEstimate(flops=1 << 10, bytes_accessed=1 << 20, transcendentals=0),
        name="spread",
    )(prompt_latent)
    keys = lax.all_to_all(spread, "z", 0, 0, tiled=True)

    by_head = jnp.transpose(prefill_query, (1, 0, 2))
    rope = by_head[:, :, NOPE:]
    packed = jnp.concatenate(
        [by_head[:, :, :NOPE], jnp.concatenate([rope[:, :32], rope[:, 32:]], axis=2)], axis=1
    )
    visiting = [packed] + [None] * 3
    for k in (2, 1, 3):
        visiting[k] = trade(packed, "yh", k, 4)
    tile = jax.ShapeDtypeStruct((40, width), bf)
    near, following, far_two = small(
        prep_kernel,
        [tile, tile, jax.ShapeDtypeStruct((80, width), bf)],
        [decode_query, w_uk, hidden_new, w_down.T],
        0,
        [pltpu.VMEM((160, width), jnp.float32)],
    )
    from_two = trade(far_two, "x", 2, 4)
    relay = jnp.concatenate([following, from_two[40:]], axis=0)
    from_one = trade(relay, "x", 1, 4)
    got = (near, from_one, from_two)
    raw_here = near[32:].astype(jnp.float32) + from_two[32:40].astype(jnp.float32)
    raw_here = raw_here + from_one[32:40].astype(jnp.float32) + from_one[72:].astype(jnp.float32)
    raw_here = raw_here + jnp.pad(kv_gain[None], ((5, 2), (0, width - KV_RANK)))
    raw_here = raw_here + jnp.pad(lengths.astype(jnp.float32)[None], ((6, 1), (0, width - 4)))
    raw_there = trade(raw_here, "yl", 1, 2)
    rows = small(
        pack_kernel,
        jax.ShapeDtypeStruct((512, width), bf),
        [owner_slot.reshape(1, 256), jnp.transpose(decode_latent, (1, 2, 0))],
    ).reshape(64, 8, width)

    keys, rows = fence((keys, rows))
    other_keys = trade(keys, "c", 1, 2)
    cache = lax.all_to_all(rows, CTX, 0, 0, tiled=True)

    chunk, key = pltpu.VMEM((8, 96, 128), bf), pltpu.VMEM((8, 96, width), bf)
    vmem = pl.BlockSpec(memory_space=pltpu.VMEM)
    parts = pl.pallas_call(
        flash_kernel,
        out_shape=[jax.ShapeDtypeStruct((512 + 16, 128), bf)] * 4,
        in_specs=[pl.BlockSpec(memory_space=pltpu.SMEM)] + [hbm] * 6 + [vmem] * 2,
        out_specs=[hbm] * 4,
        scratch_shapes=[chunk] * 4
        + [key] * 2
        + [pltpu.VMEM((512 + 16, 128), bf)] * 4
        + [pltpu.SemaphoreType.DMA((10,))],
        compiler_params=pltpu.CompilerParams(vmem_limit_bytes=28 << 20),
        cost_estimate=pl.CostEstimate(
            flops=4 * 2 * 512 * 1536 * 1100, bytes_accessed=4 << 20, transcendentals=1 << 22
        ),
        name="flash",
    )(span_start, *visiting, keys, other_keys, w_uk, w_uv)
    parts = list(parts)
    for k in (2, 1, 3):
        parts[k] = trade(parts[k], "yh", k, 4)

    mixed = small(
        attend_kernel,
        jax.ShapeDtypeStruct((4, 32, KV_RANK), bf),
        [*got, raw_here, raw_there, cache.reshape(512, width)],
    )
    mixed = lax.all_to_all(mixed, "x", 0, 0, tiled=True)
    mixed, merged = fence((mixed, merge(parts)))
    decode_out = small(finish_kernel, jax.ShapeDtypeStruct((4, 4, 8, 128), bf), [mixed, w_uv])
    prefill_out = merged.reshape(queries, heads_here, 128)
    return (prefill_out, decode_out)


def solution(mesh):
    fine = Mesh(mesh.devices.reshape(8, 4, 2, 4, 2), ("z", "yh", "c", "x", "yl"))
    in_specs = (
        P(CTX, None),
        P(CTX, HEAD, None),
        P(),
        P(HEAD, None, None),
        P(HEAD, None, None),
        P(None, CTX, None),
        P(),
        P(CTX),
        P(None, CTX, HEAD),
        P(None, CTX, HEAD, None),
        P(HEAD, None),
        P(),
    )
    out_specs = (P(CTX, HEAD, None), P(None, CTX, HEAD, None))
    return jax.shard_map(layer, mesh=fine, in_specs=in_specs, out_specs=out_specs, check_vma=False)
```

```python
import jax
import jax.numpy as jnp
from jax import lax
from jax.experimental import pallas as pl
from jax.experimental.pallas import tpu as pltpu
from jax.sharding import Mesh
from jax.sharding import PartitionSpec as P


KV_RANK = 512
ROPE = 64
NOPE = 128
LOG2E = 1.4426950408889634
SCALE = (NOPE + ROPE) ** (-0.5)
CTX = ("z", "yh", "c")
HEAD = ("x", "yl")


def split3(v):
    hi = v.astype(jnp.bfloat16)
    rest = v - hi.astype(jnp.float32)
    mid = rest.astype(jnp.bfloat16)
    low = (rest - mid.astype(jnp.float32)).astype(jnp.bfloat16)
    return hi, mid, low


def flash_kernel(start, q0, q1, q2, q3, k1_hbm, k2_hbm, wuk_ref, wuv_ref, *refs):
    targets, held, outs, full_keys, sems = refs[:4], refs[4:10], refs[10:14], refs[14:16], refs[16]
    loads = [
        pltpu.make_async_copy(m, h, sems.at[i])
        for i, (m, h) in enumerate(zip((q0, q1, q2, q3, k1_hbm, k2_hbm), held))
    ]
    for load in loads:
        load.start()
    queries, k1_ref, k2_ref = held[:4], held[4], held[5]
    z, yh, c = lax.axis_index("z"), lax.axis_index("yh"), lax.axis_index("c")
    j = lax.broadcasted_iota(jnp.int32, (1, 768), 1)
    blk = (j * 683) >> 16
    kpos = blk * 768 + (j - blk * 96) + yh * 192
    where1, where2 = kpos + c * 96, kpos + (1 - c) * 96
    row = lax.broadcasted_iota(jnp.int32, (512, 1), 0)
    source = ((row >> 6) & 3) ^ yh
    qpos = start[0] + ((source + z * 4) * 2 + c) * 64 + (row & 63)
    scale = SCALE * LOG2E
    keys = []
    lines = [[], [], [], []]

    def score(b):
        rows = []
        for h in (2 * b, 2 * b + 1):
            nope = jnp.concatenate([q[h, :64, :] for q in queries], axis=0)
            a = jnp.dot(nope, wuk_ref[h], preferred_element_type=jnp.float32)
            ropes = []
            for q in queries:
                pair = q[h, 64:, :]
                ropes += [pair[:, :64], pair[:, 64:]]
            rope = jnp.concatenate(ropes, axis=0)
            rows.append(jnp.concatenate([a.astype(jnp.bfloat16), rope], axis=1))
        full = jnp.concatenate(rows, axis=0)
        if not keys:
            for load, ref, whole in zip(loads[4:], (k1_ref, k2_ref), full_keys):
                load.wait()
                for n in range(8):
                    at = n * 96
                    for t in range(4):
                        whole[at : at + 96, t * 128 : (t + 1) * 128] = ref[n, t * 96 : (t + 1) * 96, :]
                    pair = ref[n, 384:, :]
                    whole[at : at + 48, KV_RANK:] = pair[:, :64]
                    whole[at + 48 : at + 96, KV_RANK:] = pair[:, 64:]
                keys.append(whole[...])
        return [lax.dot_general(full, k, NT, preferred_element_type=jnp.float32) for k in keys]

    def weigh(s):
        s1 = jnp.where(where1 <= qpos, s[0], -1e30)
        s2 = jnp.where(where2 <= qpos, s[1], -1e30)
        top = jnp.maximum(jnp.max(s1, axis=1, keepdims=True), jnp.max(s2, axis=1, keepdims=True))
        p1 = jnp.exp2((s1 - top) * scale)
        p2 = jnp.exp2((s2 - top) * scale)
        total = jnp.sum(p1, axis=1, keepdims=True) + jnp.sum(p2, axis=1, keepdims=True)
        lse = top * scale + jnp.log2(total)
        return p1.astype(jnp.bfloat16), p2.astype(jnp.bfloat16), total, lse

    def mix(b, p1, p2, total, lse):
        acc = jnp.dot(p1, keys[0][:, :KV_RANK], preferred_element_type=jnp.float32)
        acc = acc + jnp.dot(p2, keys[1][:, :KV_RANK], preferred_element_type=jnp.float32)
        mixed = (acc * (1.0 / total)).astype(jnp.bfloat16)
        for n in (0, 1):
            h = 2 * b + n
            o = jnp.dot(
                mixed[n * 256 : (n + 1) * 256], wuv_ref[h], preferred_element_type=jnp.float32
            ).astype(jnp.bfloat16)
            for k in range(4):
                outs[k][h * 64 : (h + 1) * 64, :] = o[k * 64 : (k + 1) * 64]
        flat = jnp.transpose(jnp.broadcast_to(lse, (512, 128)))[0:1, :]
        for k in range(4):
            at = k * 64
            lines[k].append(
                jnp.concatenate([flat[:, at : at + 64], flat[:, at + 256 : at + 320]], axis=1)
            )

    for load in loads[:4]:
        load.wait()
    s = score(0)
    for b in range(4):
        following = score(b + 1) if b < 3 else None
        mix(b, *weigh(s))
        s = following
    stores = []
    for k in (2, 1, 3, 0):
        hi, mid, low = split3(jnp.concatenate(lines[k], axis=0))
        outs[k][512:, :] = jnp.concatenate([hi, mid, low, jnp.zeros_like(hi)], axis=0)
        stores.append(pltpu.make_async_copy(outs[k], targets[k], sems.at[6 + k]))
        stores[-1].start()
    for store in stores:
        store.wait()


def merge_kernel(a_ref, b_ref, c_ref, d_ref, out_ref):
    parts = [a_ref, b_ref, c_ref, d_ref]
    weights = []
    for ref in parts:
        tail = ref[512:, :].astype(jnp.float32)
        weights.append(tail[0:4] + tail[4:8] + tail[8:12])
    top = jnp.maximum(jnp.maximum(weights[0], weights[1]), jnp.maximum(weights[2], weights[3]))
    weights = [jnp.exp2(w - top) for w in weights]
    inv = 1.0 / (weights[0] + weights[1] + weights[2] + weights[3])
    weights = [w * inv for w in weights]
    merged = []
    for i in range(4):
        total = jnp.zeros((128, 128), jnp.float32)
        for w, ref in zip(weights, parts):
            col = jnp.transpose(jnp.broadcast_to(w[i : i + 1, :], (128, 128)))
            total = total + col * ref[i * 128 : (i + 1) * 128, :].astype(jnp.float32)
        merged.append(total.astype(jnp.bfloat16))
    by_head = jnp.concatenate(merged, axis=0)
    row = lax.broadcasted_iota(jnp.int32, (512, 512), 0)
    col = lax.broadcasted_iota(jnp.int32, (512, 512), 1)
    pick = jnp.where(((row & 7) * 64 + (row >> 3)) == col, 1.0, 0.0).astype(jnp.bfloat16)
    out_ref[...] = jnp.dot(pick, by_head, preferred_element_type=jnp.float32).astype(jnp.bfloat16)


def small(kernel, outs, ins, scalars=0, scratch=(), limit=10, flops=1 << 27):
    vm = pl.BlockSpec(memory_space=pltpu.VMEM)
    sm = pl.BlockSpec(memory_space=pltpu.SMEM)
    return pl.pallas_call(
        kernel,
        out_shape=outs,
        in_specs=[sm] * scalars + [vm] * (len(ins) - scalars),
        out_specs=jax.tree.map(lambda _: vm, outs),
        scratch_shapes=scratch,
        compiler_params=pltpu.CompilerParams(vmem_limit_bytes=limit << 20),
        cost_estimate=pl.CostEstimate(flops=flops, bytes_accessed=1 << 20, transcendentals=1 << 12),
    )(*ins)


def merge(parts):
    return small(merge_kernel, jax.ShapeDtypeStruct((512, 128), jnp.bfloat16), parts)


NT = (((1,), (1,)), ((), ()))


def head_rows(count):
    return lax.broadcasted_iota(jnp.int32, (count, 1), 0) & 7


def prep_kernel(q_ref, wuk_ref, hid_ref, wd_ref, *refs):
    near, next_, far, rows = refs
    outs = (near, next_, far.at[:40], far.at[40:])
    q = q_ref[...].reshape(128, NOPE + ROPE)
    nope = q[:, :NOPE].astype(jnp.float32)
    head = head_rows(128)
    acc = jnp.zeros((128, KV_RANK), jnp.float32)
    for h in range(8):
        mine = jnp.where(head == h, nope, 0.0).astype(jnp.bfloat16)
        acc = acc + jnp.dot(mine, wuk_ref[h], preferred_element_type=jnp.float32)
    rows[:128, :KV_RANK] = acc
    rows[:128, KV_RANK:] = q[:, NOPE:].astype(jnp.float32)
    hidden = jnp.concatenate([hid_ref[t].astype(jnp.float32) for t in range(4)], axis=0)
    raw = lax.dot_general(
        hidden.astype(jnp.bfloat16), wd_ref[...], NT, preferred_element_type=jnp.float32
    ).astype(jnp.bfloat16)
    o = lax.broadcasted_iota(jnp.int32, (32, 16), 0)
    n = lax.broadcasted_iota(jnp.int32, (32, 16), 1)
    pick = jnp.where(((o & 7) * 4 + (o >> 3) == n) & ((o & 7) < 4), 1.0, 0.0)
    rows[128:, :] = jnp.dot(pick.astype(jnp.bfloat16), raw, preferred_element_type=jnp.float32)
    for k in range(4):
        r = lax.axis_index("x") ^ k
        for s in range(4):
            at = pl.multiple_of((s * 4 + r) * 8, 8)
            outs[k][s * 8 : s * 8 + 8, :] = rows[pl.ds(at, 8), :].astype(jnp.bfloat16)
        at = pl.multiple_of(128 + r * 8, 8)
        outs[k][32:40, :] = rows[pl.ds(at, 8), :].astype(jnp.bfloat16)


def pack_kernel(owner_ref, x_ref, out_ref):
    row = lax.broadcasted_iota(jnp.int32, (512, 256), 0)
    hit = owner_ref[...] == ((row >> 3) * 4 + lax.axis_index("x"))
    acc = jnp.zeros((512, KV_RANK + ROPE), jnp.float32)
    for j in range(4):
        pick = jnp.where(hit & ((row & 7) == j), 1.0, 0.0).astype(jnp.bfloat16)
        acc = acc + lax.dot_general(pick, x_ref[j], NT, preferred_element_type=jnp.float32)
    out_ref[...] = acc.astype(jnp.bfloat16)


def spread_kernel(x_ref, out_ref, held, sems):
    for t in range(4):
        held[t * 96 : (t + 1) * 96, :] = x_ref[:, t * 128 : (t + 1) * 128]
    held[384:, :] = jnp.concatenate([x_ref[:48, KV_RANK:], x_ref[48:, KV_RANK:]], axis=1)
    moves = [pltpu.make_async_copy(held, out_ref.at[i], sems.at[i]) for i in range(8)]
    for move in moves:
        move.start()
    for move in moves:
        move.wait()


def attend_kernel(p0, p13, p2, raw_a, raw_b, cache_ref, out_ref):
    lane = lax.broadcasted_iota(jnp.int32, (1, KV_RANK + ROPE), 1)
    length = jnp.where(lane == lax.axis_index("x"), raw_a[6:7, :], 0.0)
    length = jnp.sum(length, axis=1, keepdims=True).astype(jnp.int32)
    raw = raw_a[...] + raw_b[...]
    front = raw[:, :KV_RANK]
    factor = lax.rsqrt(jnp.mean(front * front, axis=1, keepdims=True) + 1e-06)
    fresh = jnp.concatenate([front * factor * raw_a[5:6, :KV_RANK], raw[:, KV_RANK:]], axis=1)
    fresh = fresh.astype(jnp.bfloat16)
    q = jnp.concatenate([p0[:32], p13[:32], p2[:32], p13[40:72]], axis=0)
    cache = cache_ref[...]
    s1 = lax.dot_general(q, cache, NT, preferred_element_type=jnp.float32)
    s2 = lax.dot_general(q, fresh, NT, preferred_element_type=jnp.float32)
    j = lax.broadcasted_iota(jnp.int32, (128, 512), 1)
    held = ((j & 7) < 4) & ((j >> 3) * 4 + (j & 7) < length)
    s1 = jnp.where(held, s1, -1e30)
    step = (lax.broadcasted_iota(jnp.int32, (128, 8), 0) >> 3) & 3
    s2 = jnp.where(lax.broadcasted_iota(jnp.int32, (128, 8), 1) <= step, s2, -1e30)
    top = jnp.maximum(jnp.max(s1, axis=1, keepdims=True), jnp.max(s2, axis=1, keepdims=True))
    c = SCALE * LOG2E
    p_c = jnp.exp2((s1 - top) * c)
    p_n = jnp.exp2((s2 - top) * c)
    total = jnp.sum(p_c, axis=1, keepdims=True) + jnp.sum(p_n, axis=1, keepdims=True)
    acc = jnp.dot(p_c.astype(jnp.bfloat16), cache[:, :KV_RANK], preferred_element_type=jnp.float32)
    acc = acc + jnp.dot(
        p_n.astype(jnp.bfloat16), fresh[:, :KV_RANK], preferred_element_type=jnp.float32
    )
    mixed = (acc / total).astype(jnp.bfloat16)
    for k in range(4):
        out_ref[lax.axis_index("x") ^ k] = mixed[k * 32 : (k + 1) * 32]


def finish_kernel(m_ref, wuv_ref, out_ref):
    m = m_ref[...].reshape(128, KV_RANK).astype(jnp.float32)
    head = head_rows(128)
    acc = jnp.zeros((128, 128), jnp.float32)
    for h in range(8):
        mine = jnp.where(head == h, m, 0.0).astype(jnp.bfloat16)
        acc = acc + jnp.dot(mine, wuv_ref[h], preferred_element_type=jnp.float32)
    for r in range(4):
        for s in range(4):
            at = (r * 4 + s) * 8
            out_ref[s, r] = acc[at : at + 8].astype(jnp.bfloat16)


def trade(v, axis, k, n):
    return lax.ppermute(v, axis, [(i, i ^ k) for i in range(n)])


def layer(
    prompt_latent,
    prefill_query,
    span_start,
    w_uk,
    w_uv,
    decode_latent,
    owner_slot,
    lengths,
    hidden_new,
    decode_query,
    w_down,
    kv_gain,
):
    heads_here = w_uk.shape[0]
    queries = prefill_query.shape[0]
    width = prompt_latent.shape[1]
    bf = jnp.bfloat16
    fence = lax.optimization_barrier
    hbm = pl.BlockSpec(memory_space=pltpu.HBM)
    spread = pl.pallas_call(
        spread_kernel,
        out_shape=jax.ShapeDtypeStruct((8, 432, 128), bf),
        in_specs=[pl.BlockSpec(memory_space=pltpu.VMEM)],
        out_specs=hbm,
        scratch_shapes=[pltpu.VMEM((432, 128), bf), pltpu.SemaphoreType.DMA((8,))],
        compiler_params=pltpu.CompilerParams(vmem_limit_bytes=4 << 20),
        cost_estimate=pl.CostEstimate(flops=1 << 10, bytes_accessed=1 << 20, transcendentals=0),
        name="spread",
    )(prompt_latent)
    keys = lax.all_to_all(spread, "z", 0, 0, tiled=True)

    by_head = jnp.transpose(prefill_query, (1, 0, 2))
    rope = by_head[:, :, NOPE:]
    packed = jnp.concatenate(
        [by_head[:, :, :NOPE], jnp.concatenate([rope[:, :32], rope[:, 32:]], axis=2)], axis=1
    )
    visiting = [packed] + [None] * 3
    for k in (2, 1, 3):
        visiting[k] = trade(packed, "yh", k, 4)
    tile = jax.ShapeDtypeStruct((40, width), bf)
    near, following, far_two = small(
        prep_kernel,
        [tile, tile, jax.ShapeDtypeStruct((80, width), bf)],
        [decode_query, w_uk, hidden_new, w_down.T],
        0,
        [pltpu.VMEM((160, width), jnp.float32)],
    )
    from_two = trade(far_two, "x", 2, 4)
    relay = jnp.concatenate([following, from_two[40:]], axis=0)
    from_one = trade(relay, "x", 1, 4)
    got = (near, from_one, from_two)
    raw_here = near[32:].astype(jnp.float32) + from_two[32:40].astype(jnp.float32)
    raw_here = raw_here + from_one[32:40].astype(jnp.float32) + from_one[72:].astype(jnp.float32)
    raw_here = raw_here + jnp.pad(kv_gain[None], ((5, 2), (0, width - KV_RANK)))
    raw_here = raw_here + jnp.pad(lengths.astype(jnp.float32)[None], ((6, 1), (0, width - 4)))
    raw_there = trade(raw_here, "yl", 1, 2)
    rows = small(
        pack_kernel,
        jax.ShapeDtypeStruct((512, width), bf),
        [owner_slot.reshape(1, 256), jnp.transpose(decode_latent, (1, 2, 0))],
    ).reshape(64, 8, width)

    keys, rows = fence((keys, rows))
    other_keys = trade(keys, "c", 1, 2)
    cache = lax.all_to_all(rows, CTX, 0, 0, tiled=True)

    chunk, key = pltpu.VMEM((8, 96, 128), bf), pltpu.VMEM((8, 432, 128), bf)
    vmem = pl.BlockSpec(memory_space=pltpu.VMEM)
    parts = pl.pallas_call(
        flash_kernel,
        out_shape=[jax.ShapeDtypeStruct((512 + 16, 128), bf)] * 4,
        in_specs=[pl.BlockSpec(memory_space=pltpu.SMEM)] + [hbm] * 6 + [vmem] * 2,
        out_specs=[hbm] * 4,
        scratch_shapes=[chunk] * 4
        + [key] * 2
        + [pltpu.VMEM((512 + 16, 128), bf)] * 4
        + [pltpu.VMEM((768, width), bf)] * 2
        + [pltpu.SemaphoreType.DMA((10,))],
        compiler_params=pltpu.CompilerParams(vmem_limit_bytes=28 << 20),
        cost_estimate=pl.CostEstimate(
            flops=4 * 2 * 512 * 1536 * 1100, bytes_accessed=4 << 20, transcendentals=1 << 22
        ),
        name="flash",
    )(span_start, *visiting, keys, other_keys, w_uk, w_uv)
    parts = list(parts)
    for k in (2, 1, 3):
        parts[k] = trade(parts[k], "yh", k, 4)

    mixed = small(
        attend_kernel,
        jax.ShapeDtypeStruct((4, 32, KV_RANK), bf),
        [*got, raw_here, raw_there, cache.reshape(512, width)],
    )
    mixed = lax.all_to_all(mixed, "x", 0, 0, tiled=True)
    mixed, merged = fence((mixed, merge(parts)))
    decode_out = small(finish_kernel, jax.ShapeDtypeStruct((4, 4, 8, 128), bf), [mixed, w_uv])
    prefill_out = merged.reshape(queries, heads_here, 128)
    return (prefill_out, decode_out)


def solution(mesh):
    fine = Mesh(mesh.devices.reshape(8, 4, 2, 4, 2), ("z", "yh", "c", "x", "yl"))
    in_specs = (
        P(CTX, None),
        P(CTX, HEAD, None),
        P(),
        P(HEAD, None, None),
        P(HEAD, None, None),
        P(None, CTX, None),
        P(),
        P(CTX),
        P(None, CTX, HEAD),
        P(None, CTX, HEAD, None),
        P(HEAD, None),
        P(),
    )
    out_specs = (P(CTX, HEAD, None), P(None, CTX, HEAD, None))
    return jax.shard_map(layer, mesh=fine, in_specs=in_specs, out_specs=out_specs, check_vma=False)
```

```python
import jax
import jax.numpy as jnp
from jax import lax
from jax.experimental import pallas as pl
from jax.experimental.pallas import tpu as pltpu
from jax.sharding import Mesh
from jax.sharding import PartitionSpec as P


KV_RANK = 512
ROPE = 64
NOPE = 128
LOG2E = 1.4426950408889634
SCALE = (NOPE + ROPE) ** (-0.5)
CTX = ("z", "yh", "c")
HEAD = ("x", "yl")


def split3(v):
    hi = v.astype(jnp.bfloat16)
    rest = v - hi.astype(jnp.float32)
    mid = rest.astype(jnp.bfloat16)
    low = (rest - mid.astype(jnp.float32)).astype(jnp.bfloat16)
    return hi, mid, low


def flash_kernel(start, q0, q1, q2, q3, k1_hbm, k2_hbm, wuk_ref, wuv_ref, *refs):
    targets, held, outs, full_keys, sems = refs[:4], refs[4:10], refs[10:14], refs[14:16], refs[16]
    loads = [
        pltpu.make_async_copy(m, h, sems.at[i])
        for i, (m, h) in enumerate(zip((q0, q1, q2, q3, k1_hbm, k2_hbm), held))
    ]
    for load in loads:
        load.start()
    queries, k1_ref, k2_ref = held[:4], held[4], held[5]
    z, yh, c = lax.axis_index("z"), lax.axis_index("yh"), lax.axis_index("c")
    j = lax.broadcasted_iota(jnp.int32, (1, 768), 1)
    blk = (j * 683) >> 16
    kpos = blk * 768 + (j - blk * 96) + yh * 192
    where1, where2 = kpos + c * 96, kpos + (1 - c) * 96
    row = lax.broadcasted_iota(jnp.int32, (512, 1), 0)
    source = ((row >> 6) & 3) ^ yh
    qpos = start[0] + ((source + z * 4) * 2 + c) * 64 + (row & 63)
    scale = SCALE * LOG2E
    keys = []
    lines = [[], [], [], []]

    def score(b):
        rows = []
        for h in (2 * b, 2 * b + 1):
            nope = jnp.concatenate([q[h, :64, :] for q in queries], axis=0)
            a = jnp.dot(nope, wuk_ref[h], preferred_element_type=jnp.float32)
            ropes = []
            for q in queries:
                pair = q[h, 64:, :]
                ropes += [pair[:, :64], pair[:, 64:]]
            rope = jnp.concatenate(ropes, axis=0)
            rows.append(jnp.concatenate([a.astype(jnp.bfloat16), rope], axis=1))
        full = jnp.concatenate(rows, axis=0)
        if not keys:
            for load, ref, whole in zip(loads[4:], (k1_ref, k2_ref), full_keys):
                load.wait()
                for n in range(8):
                    at = n * 96
                    for t in range(4):
                        whole[at : at + 96, t * 128 : (t + 1) * 128] = ref[n, t * 96 : (t + 1) * 96, :]
                    pair = ref[n, 384:, :]
                    whole[at : at + 48, KV_RANK:] = pair[:, :64]
                    whole[at + 48 : at + 96, KV_RANK:] = pair[:, 64:]
                keys.append(whole[...])
        return [lax.dot_general(full, k, NT, preferred_element_type=jnp.float32) for k in keys]

    def weigh(s):
        s1 = jnp.where(where1 <= qpos, s[0], -1e30)
        s2 = jnp.where(where2 <= qpos, s[1], -1e30)
        top = jnp.maximum(jnp.max(s1, axis=1, keepdims=True), jnp.max(s2, axis=1, keepdims=True))
        p1 = jnp.exp2((s1 - top) * scale)
        p2 = jnp.exp2((s2 - top) * scale)
        total = jnp.sum(p1, axis=1, keepdims=True) + jnp.sum(p2, axis=1, keepdims=True)
        lse = top * scale + jnp.log2(total)
        return p1.astype(jnp.bfloat16), p2.astype(jnp.bfloat16), total, lse

    def mix(b, p1, p2, total, lse):
        acc = jnp.dot(p1, keys[0][:, :KV_RANK], preferred_element_type=jnp.float32)
        acc = acc + jnp.dot(p2, keys[1][:, :KV_RANK], preferred_element_type=jnp.float32)
        mixed = (acc * (1.0 / total)).astype(jnp.bfloat16)
        for n in (0, 1):
            h = 2 * b + n
            o = jnp.dot(
                mixed[n * 256 : (n + 1) * 256], wuv_ref[h], preferred_element_type=jnp.float32
            ).astype(jnp.bfloat16)
            for k in range(4):
                outs[k][h * 64 : (h + 1) * 64, :] = o[k * 64 : (k + 1) * 64]
        flat = jnp.transpose(jnp.broadcast_to(lse, (512, 128)))[0:1, :]
        for k in range(4):
            at = k * 64
            lines[k].append(
                jnp.concatenate([flat[:, at : at + 64], flat[:, at + 256 : at + 320]], axis=1)
            )

    for load in loads[:4]:
        load.wait()
    s = score(0)
    for b in range(4):
        following = score(b + 1) if b < 3 else None
        mix(b, *weigh(s))
        s = following
    stores = []
    for k in (2, 1, 3, 0):
        hi, mid, low = split3(jnp.concatenate(lines[k], axis=0))
        outs[k][512:, :] = jnp.concatenate([hi, mid, low, jnp.zeros_like(hi)], axis=0)
        stores.append(pltpu.make_async_copy(outs[k], targets[k], sems.at[6 + k]))
        stores[-1].start()
    for store in stores:
        store.wait()


def merge_kernel(a_ref, b_ref, c_ref, d_ref, out_ref):
    parts = [a_ref, b_ref, c_ref, d_ref]
    weights = []
    for ref in parts:
        tail = ref[512:, :].astype(jnp.float32)
        weights.append(tail[0:4] + tail[4:8] + tail[8:12])
    top = jnp.maximum(jnp.maximum(weights[0], weights[1]), jnp.maximum(weights[2], weights[3]))
    weights = [jnp.exp2(w - top) for w in weights]
    inv = 1.0 / (weights[0] + weights[1] + weights[2] + weights[3])
    weights = [w * inv for w in weights]
    merged = []
    for i in range(4):
        total = jnp.zeros((128, 128), jnp.float32)
        for w, ref in zip(weights, parts):
            col = jnp.transpose(jnp.broadcast_to(w[i : i + 1, :], (128, 128)))
            total = total + col * ref[i * 128 : (i + 1) * 128, :].astype(jnp.float32)
        merged.append(total.astype(jnp.bfloat16))
    by_head = jnp.concatenate(merged, axis=0)
    row = lax.broadcasted_iota(jnp.int32, (512, 512), 0)
    col = lax.broadcasted_iota(jnp.int32, (512, 512), 1)
    pick = jnp.where(((row & 7) * 64 + (row >> 3)) == col, 1.0, 0.0).astype(jnp.bfloat16)
    out_ref[...] = jnp.dot(pick, by_head, preferred_element_type=jnp.float32).astype(jnp.bfloat16)


def small(kernel, outs, ins, scalars=0, scratch=(), limit=10, flops=1 << 27):
    vm = pl.BlockSpec(memory_space=pltpu.VMEM)
    sm = pl.BlockSpec(memory_space=pltpu.SMEM)
    return pl.pallas_call(
        kernel,
        out_shape=outs,
        in_specs=[sm] * scalars + [vm] * (len(ins) - scalars),
        out_specs=jax.tree.map(lambda _: vm, outs),
        scratch_shapes=scratch,
        compiler_params=pltpu.CompilerParams(vmem_limit_bytes=limit << 20),
        cost_estimate=pl.CostEstimate(flops=flops, bytes_accessed=1 << 20, transcendentals=1 << 12),
    )(*ins)


def merge(parts):
    return small(merge_kernel, jax.ShapeDtypeStruct((512, 128), jnp.bfloat16), parts)


NT = (((1,), (1,)), ((), ()))


def head_rows(count):
    return lax.broadcasted_iota(jnp.int32, (count, 1), 0) & 7


def prep_kernel(q_ref, wuk_ref, hid_ref, wd_ref, *refs):
    near, next_, far, rows = refs
    outs = (near, next_, far.at[:40], far.at[40:])
    q = q_ref[...].reshape(128, NOPE + ROPE)
    nope = q[:, :NOPE].astype(jnp.float32)
    head = head_rows(128)
    acc = jnp.zeros((128, KV_RANK), jnp.float32)
    for h in range(8):
        mine = jnp.where(head == h, nope, 0.0).astype(jnp.bfloat16)
        acc = acc + jnp.dot(mine, wuk_ref[h], preferred_element_type=jnp.float32)
    rows[:128, :KV_RANK] = acc
    rows[:128, KV_RANK:] = q[:, NOPE:].astype(jnp.float32)
    hidden = jnp.concatenate([hid_ref[t].astype(jnp.float32) for t in range(4)], axis=0)
    raw = lax.dot_general(
        hidden.astype(jnp.bfloat16), wd_ref[...], NT, preferred_element_type=jnp.float32
    ).astype(jnp.bfloat16)
    o = lax.broadcasted_iota(jnp.int32, (32, 16), 0)
    n = lax.broadcasted_iota(jnp.int32, (32, 16), 1)
    pick = jnp.where(((o & 7) * 4 + (o >> 3) == n) & ((o & 7) < 4), 1.0, 0.0)
    rows[128:, :] = jnp.dot(pick.astype(jnp.bfloat16), raw, preferred_element_type=jnp.float32)
    for k in range(4):
        r = lax.axis_index("x") ^ k
        for s in range(4):
            at = pl.multiple_of((s * 4 + r) * 8, 8)
            outs[k][s * 8 : s * 8 + 8, :] = rows[pl.ds(at, 8), :].astype(jnp.bfloat16)
        at = pl.multiple_of(128 + r * 8, 8)
        outs[k][32:40, :] = rows[pl.ds(at, 8), :].astype(jnp.bfloat16)


def pack_kernel(owner_ref, x_ref, out_ref):
    row = lax.broadcasted_iota(jnp.int32, (256, 256), 0)
    hit = owner_ref[...] == ((row >> 2) * 4 + lax.axis_index("x"))
    acc = jnp.zeros((256, KV_RANK + ROPE), jnp.float32)
    for j in range(4):
        pick = jnp.where(hit & ((row & 3) == j), 1.0, 0.0).astype(jnp.bfloat16)
        acc = acc + lax.dot_general(pick, x_ref[j], NT, preferred_element_type=jnp.float32)
    out_ref[...] = acc.astype(jnp.bfloat16)


def spread_kernel(x_ref, out_ref, held, sems):
    for t in range(4):
        held[t * 96 : (t + 1) * 96, :] = x_ref[:, t * 128 : (t + 1) * 128]
    held[384:, :] = jnp.concatenate([x_ref[:48, KV_RANK:], x_ref[48:, KV_RANK:]], axis=1)
    moves = [pltpu.make_async_copy(held, out_ref.at[i], sems.at[i]) for i in range(8)]
    for move in moves:
        move.start()
    for move in moves:
        move.wait()


def attend_kernel(p0, p13, p2, raw_a, raw_b, cache_ref, out_ref):
    lane = lax.broadcasted_iota(jnp.int32, (1, KV_RANK + ROPE), 1)
    length = jnp.where(lane == lax.axis_index("x"), raw_a[6:7, :], 0.0)
    length = jnp.sum(length, axis=1, keepdims=True).astype(jnp.int32)
    raw = raw_a[...] + raw_b[...]
    front = raw[:, :KV_RANK]
    factor = lax.rsqrt(jnp.mean(front * front, axis=1, keepdims=True) + 1e-06)
    fresh = jnp.concatenate([front * factor * raw_a[5:6, :KV_RANK], raw[:, KV_RANK:]], axis=1)
    fresh = fresh.astype(jnp.bfloat16)
    q = jnp.concatenate([p0[:32], p13[:32], p2[:32], p13[40:72]], axis=0)
    cache = cache_ref[...]
    s1 = lax.dot_general(q, cache, NT, preferred_element_type=jnp.float32)
    s2 = lax.dot_general(q, fresh, NT, preferred_element_type=jnp.float32)
    j = lax.broadcasted_iota(jnp.int32, (128, 256), 1)
    s1 = jnp.where(j < length, s1, -1e30)
    step = (lax.broadcasted_iota(jnp.int32, (128, 8), 0) >> 3) & 3
    s2 = jnp.where(lax.broadcasted_iota(jnp.int32, (128, 8), 1) <= step, s2, -1e30)
    top = jnp.maximum(jnp.max(s1, axis=1, keepdims=True), jnp.max(s2, axis=1, keepdims=True))
    c = SCALE * LOG2E
    p_c = jnp.exp2((s1 - top) * c)
    p_n = jnp.exp2((s2 - top) * c)
    total = jnp.sum(p_c, axis=1, keepdims=True) + jnp.sum(p_n, axis=1, keepdims=True)
    acc = jnp.dot(p_c.astype(jnp.bfloat16), cache[:, :KV_RANK], preferred_element_type=jnp.float32)
    acc = acc + jnp.dot(
        p_n.astype(jnp.bfloat16), fresh[:, :KV_RANK], preferred_element_type=jnp.float32
    )
    mixed = (acc / total).astype(jnp.bfloat16)
    for k in range(4):
        out_ref[lax.axis_index("x") ^ k] = mixed[k * 32 : (k + 1) * 32]


def finish_kernel(m_ref, wuv_ref, out_ref):
    m = m_ref[...].reshape(128, KV_RANK).astype(jnp.float32)
    head = head_rows(128)
    acc = jnp.zeros((128, 128), jnp.float32)
    for h in range(8):
        mine = jnp.where(head == h, m, 0.0).astype(jnp.bfloat16)
        acc = acc + jnp.dot(mine, wuv_ref[h], preferred_element_type=jnp.float32)
    for r in range(4):
        for s in range(4):
            at = (r * 4 + s) * 8
            out_ref[s, r] = acc[at : at + 8].astype(jnp.bfloat16)


def trade(v, axis, k, n):
    return lax.ppermute(v, axis, [(i, i ^ k) for i in range(n)])


def layer(
    prompt_latent,
    prefill_query,
    span_start,
    w_uk,
    w_uv,
    decode_latent,
    owner_slot,
    lengths,
    hidden_new,
    decode_query,
    w_down,
    kv_gain,
):
    heads_here = w_uk.shape[0]
    queries = prefill_query.shape[0]
    width = prompt_latent.shape[1]
    bf = jnp.bfloat16
    fence = lax.optimization_barrier
    hbm = pl.BlockSpec(memory_space=pltpu.HBM)
    spread = pl.pallas_call(
        spread_kernel,
        out_shape=jax.ShapeDtypeStruct((8, 432, 128), bf),
        in_specs=[pl.BlockSpec(memory_space=pltpu.VMEM)],
        out_specs=hbm,
        scratch_shapes=[pltpu.VMEM((432, 128), bf), pltpu.SemaphoreType.DMA((8,))],
        compiler_params=pltpu.CompilerParams(vmem_limit_bytes=4 << 20),
        cost_estimate=pl.CostEstimate(flops=1 << 10, bytes_accessed=1 << 20, transcendentals=0),
        name="spread",
    )(prompt_latent)
    keys = lax.all_to_all(spread, "z", 0, 0, tiled=True)

    by_head = jnp.transpose(prefill_query, (1, 0, 2))
    rope = by_head[:, :, NOPE:]
    packed = jnp.concatenate(
        [by_head[:, :, :NOPE], jnp.concatenate([rope[:, :32], rope[:, 32:]], axis=2)], axis=1
    )
    visiting = [packed] + [None] * 3
    for k in (2, 1, 3):
        visiting[k] = trade(packed, "yh", k, 4)
    tile = jax.ShapeDtypeStruct((40, width), bf)
    near, following, far_two = small(
        prep_kernel,
        [tile, tile, jax.ShapeDtypeStruct((80, width), bf)],
        [decode_query, w_uk, hidden_new, w_down.T],
        0,
        [pltpu.VMEM((160, width), jnp.float32)],
    )
    from_two = trade(far_two, "x", 2, 4)
    relay = jnp.concatenate([following, from_two[40:]], axis=0)
    from_one = trade(relay, "x", 1, 4)
    got = (near, from_one, from_two)
    raw_here = near[32:].astype(jnp.float32) + from_two[32:40].astype(jnp.float32)
    raw_here = raw_here + from_one[32:40].astype(jnp.float32) + from_one[72:].astype(jnp.float32)
    raw_here = raw_here + jnp.pad(kv_gain[None], ((5, 2), (0, width - KV_RANK)))
    raw_here = raw_here + jnp.pad(lengths.astype(jnp.float32)[None], ((6, 1), (0, width - 4)))
    raw_there = trade(raw_here, "yl", 1, 2)
    rows = small(
        pack_kernel,
        jax.ShapeDtypeStruct((256, width), bf),
        [owner_slot.reshape(1, 256), jnp.transpose(decode_latent, (1, 2, 0))],
    ).reshape(64, 4, width)

    keys, rows = fence((keys, rows))
    other_keys = trade(keys, "c", 1, 2)
    cache = lax.all_to_all(rows, CTX, 0, 0, tiled=True)

    chunk, key = pltpu.VMEM((8, 96, 128), bf), pltpu.VMEM((8, 432, 128), bf)
    vmem = pl.BlockSpec(memory_space=pltpu.VMEM)
    parts = pl.pallas_call(
        flash_kernel,
        out_shape=[jax.ShapeDtypeStruct((512 + 16, 128), bf)] * 4,
        in_specs=[pl.BlockSpec(memory_space=pltpu.SMEM)] + [hbm] * 6 + [vmem] * 2,
        out_specs=[hbm] * 4,
        scratch_shapes=[chunk] * 4
        + [key] * 2
        + [pltpu.VMEM((512 + 16, 128), bf)] * 4
        + [pltpu.VMEM((768, width), bf)] * 2
        + [pltpu.SemaphoreType.DMA((10,))],
        compiler_params=pltpu.CompilerParams(vmem_limit_bytes=28 << 20),
        cost_estimate=pl.CostEstimate(
            flops=4 * 2 * 512 * 1536 * 1100, bytes_accessed=4 << 20, transcendentals=1 << 22
        ),
        name="flash",
    )(span_start, *visiting, keys, other_keys, w_uk, w_uv)
    parts = list(parts)
    for k in (2, 1, 3):
        parts[k] = trade(parts[k], "yh", k, 4)

    mixed = small(
        attend_kernel,
        jax.ShapeDtypeStruct((4, 32, KV_RANK), bf),
        [*got, raw_here, raw_there, cache.reshape(256, width)],
    )
    mixed = lax.all_to_all(mixed, "x", 0, 0, tiled=True)
    mixed, merged = fence((mixed, merge(parts)))
    decode_out = small(finish_kernel, jax.ShapeDtypeStruct((4, 4, 8, 128), bf), [mixed, w_uv])
    prefill_out = merged.reshape(queries, heads_here, 128)
    return (prefill_out, decode_out)


def solution(mesh):
    fine = Mesh(mesh.devices.reshape(8, 4, 2, 4, 2), ("z", "yh", "c", "x", "yl"))
    in_specs = (
        P(CTX, None),
        P(CTX, HEAD, None),
        P(),
        P(HEAD, None, None),
        P(HEAD, None, None),
        P(None, CTX, None),
        P(),
        P(CTX),
        P(None, CTX, HEAD),
        P(None, CTX, HEAD, None),
        P(HEAD, None),
        P(),
    )
    out_specs = (P(CTX, HEAD, None), P(None, CTX, HEAD, None))
    return jax.shard_map(layer, mesh=fine, in_specs=in_specs, out_specs=out_specs, check_vma=False)
```
